256 devices in a mesh: grp: 8 (over z), row: 32 (over y, x, core).
Axes of the slice: x: 4, y: 4, z: 8, core: 2. Of those that a mesh axis runs over, the one named last changes fastest.
Arguments:
- gradient: float32 [8, 4096, 1024], P('grp', 'row'), may hold values from -8000 to 8000
- weight: float32 [8, 4096, 1024], P('grp', 'row'), may hold values from -0.09375 to 0.09375
- dual: float32 [8, 1024, 1024], P('grp'), may hold values from -6 to 6
Outputs:
- update: float32 [8, 4096, 1024], P('grp', 'row')
- dual_next: float32 [8, 1024, 1024], P('grp', 'row')
The draws below stay inside these ranges and needn't reach their ends.
All inputs are finite; a program needn't handle non-finite values.
Results may differ from the reference program's by a relative error of at most 0.03.
Values may be sent and summed in bfloat16 or wider, within the bound.
A program may use at most 64 MiB of HBM per device.

```python
import math
import jax
import jax.numpy as jnp
from jax import lax

ROWS = 4096
COLS = 1024
NS_STEPS = 4
MATS = 8
ROW_DEV = 128
N_ROW = 32


def draw_gradient(key, part):
    keys = jax.random.split(key, 3)
    row_scale = jnp.exp(jax.random.uniform(keys[0], (ROWS,), jnp.float32) * math.log(10.0))
    col_scale = jnp.exp(jax.random.uniform(keys[1], (COLS,), jnp.float32) * math.log(10.0))
    row_trend = jnp.exp(math.log(3.0) * jnp.arange(ROWS, dtype=jnp.float32) / ROWS)
    mat_trend = jnp.exp(math.log(3.0) * jnp.arange(MATS, dtype=jnp.float32) / max(MATS - 1, 1))
    base = jnp.clip(jax.random.normal(keys[2], (MATS, ROWS, COLS), jnp.float32), -6.0, 6.0)
    scaled = base * (row_scale * row_trend)[None, :, None] * col_scale[None, None, :]
    return (scaled * mat_trend[:, None, None]).astype(jnp.float32)


def steps_of(key, dims, shards, low, largest):
    factor_of = 1.0
    for axis_at, shards_of in shards:
        draws = jax.random.uniform(jax.random.fold_in(jax.random.fold_in(key, 6), axis_at), (shards_of,), jnp.float32, low / len(shards), largest / len(shards))
        factor_of = factor_of * jnp.repeat(jnp.exp(draws), dims[axis_at] // shards_of).reshape((-1,) + (1,) * (len(dims) - 1 - axis_at))
    return factor_of


def bell_draw(stream_key, extent, width, reach, shards=(), kind=jnp.bfloat16):
    gain = steps_of(stream_key, extent, shards, -0.22, 0.18) if shards else 1.0
    entries = jax.random.normal(stream_key, extent, jnp.float32) * width * gain
    return jnp.minimum(jnp.maximum(entries, -reach), reach).astype(kind)


def setup_inputs(seed: int = 0) -> dict:
    seeds = jax.random.split(jax.random.key(seed), 4)
    gradient = draw_gradient(jax.random.fold_in(seeds[3], 71), 0)
    weight = bell_draw(seeds[1], (MATS, ROWS, COLS), ROWS ** -0.5, 0.09375, ((0, 8), (1, 32)), jnp.float32)
    dual = bell_draw(seeds[2], (MATS, COLS, COLS), 1.0, 6.0, ((0, 8),), jnp.float32)
    return dict(gradient=gradient, weight=weight, dual=dual)


coef_a = 3.4445
coef_b = -4.775
coef_c = 2.0315
epsilon = 1e-06

def one_matrix(gradient_one, weight_one, dual_one, clip_scale):
    symmetric = 0.5 * (dual_one + dual_one.T)
    target = clip_scale * gradient_one + jnp.dot(weight_one, symmetric, precision=lax.Precision.HIGHEST, preferred_element_type=jnp.float32)
    iterate = (target * lax.rsqrt(jnp.sum(target * target) + epsilon)).astype(jnp.bfloat16)
    for step_index in range(NS_STEPS):
        blocks = iterate.reshape(N_ROW, ROW_DEV, COLS)

        def add_block(carry, block):
            partial_sum = jnp.dot(block.T, block, preferred_element_type=jnp.float32).astype(jnp.bfloat16)
            return (carry + partial_sum.astype(jnp.float32), None)
        summed, unused = lax.scan(add_block, jnp.zeros((COLS, COLS), jnp.float32), blocks)
        gram_full = summed.astype(jnp.bfloat16)
        square = jnp.dot(gram_full, gram_full, preferred_element_type=jnp.float32)
        poly_full = (coef_b * gram_full.astype(jnp.float32) + coef_c * square).astype(jnp.bfloat16)
        product = jnp.dot(iterate, poly_full, preferred_element_type=jnp.float32)
        iterate = (coef_a * iterate.astype(jnp.float32) + product).astype(jnp.bfloat16)
    iterate_wide = iterate.astype(jnp.float32)
    update = jnp.sqrt(jnp.float32(COLS)) * iterate_wide
    cross = jnp.dot(weight_one.T, iterate_wide, precision=lax.Precision.HIGHEST, preferred_element_type=jnp.float32)
    dual_next = dual_one - jnp.sqrt(jnp.float32(COLS)) * 0.5 * (cross + cross.T)
    return (update, dual_next)

def reference(gradient, weight, dual):
    grand_total = jnp.sum(gradient * gradient)
    clip_scale = jnp.minimum(jnp.float32(1.0), 0.5 * jnp.sqrt(jnp.float32(ROWS * COLS * MATS)) / jnp.sqrt(grand_total))

    def handle(items):
        return one_matrix(items[0], items[1], items[2], clip_scale)
    update, dual_next = lax.map(handle, (gradient, weight, dual))
    return (update, dual_next)
```

```python
import math

import jax
import jax.numpy as jnp
from jax import lax
from jax.experimental import pallas as pl
from jax.experimental.pallas import tpu as pltpu
from jax.sharding import Mesh
from jax.sharding import PartitionSpec as P

ROW = ("row_0", "row_1", "row_2")
MESH = pl.DeviceIdType.MESH
coef_a = 3.4445
coef_b = -4.775
coef_c = 2.0315
epsilon = 1e-06
WIN = 640
F32 = jnp.float32
BF16 = jnp.bfloat16


class Copies:
    def __init__(self, send, recv):
        self.send, self.recv, self.n = send, recv, 0

    def __call__(self, src, dst, where):
        i = self.n
        self.n += 1
        copy = pltpu.make_async_remote_copy(
            src_ref=src, dst_ref=dst, send_sem=self.send.at[i], recv_sem=self.recv.at[i],
            device_id=where, device_id_type=MESH,
        )
        copy.start()
        return copy


def turn(p, d, n):
    return lax.rem(p + d, n)


class RingSum:
    def __init__(self, copies, axis, p, part, t, u, r, h):
        self.c, self.axis, self.p, self.part, self.t, self.u, self.r, self.h = (
            copies, axis, p, part, t, u, r, h)

    def first(self):
        c, p, part, t, r, h = self.c, self.p, self.part, self.t, self.r, self.h
        right, left, far = turn(p, 1, 4), turn(p, 3, 4), turn(p, 2, 4)
        to_r, to_l = {self.axis: right}, {self.axis: left}
        lo, hi = pl.ds(0, h), pl.ds(h, h)
        self.a = c(part.at[far, lo], t.at[0], to_r)
        self.b = c(part.at[far, hi], t.at[1], to_l)
        self.e = c(part.at[right, hi], r.at[0, hi], to_r)
        self.f = c(part.at[left, lo], r.at[1, lo], to_l)

    def second(self):
        c, p, part, t, u, r, h = self.c, self.p, self.part, self.t, self.u, self.r, self.h
        right, left = turn(p, 1, 4), turn(p, 3, 4)
        lo, hi = pl.ds(0, h), pl.ds(h, h)
        self.a.wait_recv()
        u[0] = part[right, lo] + t[0]
        self.g = c(u.at[0], r.at[0, lo], {self.axis: right})
        self.b.wait_recv()
        u[1] = part[left, hi] + t[1]
        self.i = c(u.at[1], r.at[1, hi], {self.axis: left})

    def third(self):
        for copy in (self.e, self.f, self.g, self.i):
            copy.wait_recv()
        return self.part[self.p] + self.r[0] + self.r[1]

    def drain(self):
        for copy in (self.a, self.b, self.e, self.f, self.g, self.i):
            copy.wait_send()


class RingSpread:
    def __init__(self, copies, axis, p, part, h):
        self.c, self.axis, self.p, self.part, self.h = copies, axis, p, part, h

    def first(self):
        c, p, part, h = self.c, self.p, self.part, self.h
        to_r, to_l = {self.axis: turn(p, 1, 4)}, {self.axis: turn(p, 3, 4)}
        lo, hi = pl.ds(0, h), pl.ds(h, h)
        self.a = c(part.at[p, lo], part.at[p, lo], to_r)
        self.b = c(part.at[p, hi], part.at[p, hi], to_l)
        self.e = c(part.at[p, hi], part.at[p, hi], to_r)
        self.f = c(part.at[p, lo], part.at[p, lo], to_l)

    def second(self):
        c, p, part, h = self.c, self.p, self.part, self.h
        right, left = turn(p, 1, 4), turn(p, 3, 4)
        lo, hi = pl.ds(0, h), pl.ds(h, h)
        self.a.wait_recv()
        self.g = c(part.at[left, lo], part.at[left, lo], {self.axis: right})
        self.b.wait_recv()
        self.i = c(part.at[right, hi], part.at[right, hi], {self.axis: left})

    def near(self):
        self.e.wait_recv()
        self.f.wait_recv()

    def last(self):
        self.g.wait_recv()
        self.i.wait_recv()

    def drain(self):
        for copy in (self.a, self.b, self.e, self.f, self.g, self.i):
            copy.wait_send()


def gram_kernel(threshold, g_ref, w_hbm, d_hbm, t_ref, gram_ref,
                w_v, d_v, wst, wt, stat_s, stat_r, xd, pa, pb, ta, tb, ua, ub, ra, rb,
                qa, qb, ta2, tb2, ua2, ub2, ra2, rb2, fa, fb, in_sem, send, recv):
    z = lax.axis_index("grp")
    y = lax.axis_index("row_0")
    x = lax.axis_index("row_1")
    k = lax.axis_index("row_2")
    other = 1 - k
    c = Copies(send, recv)
    load_d = pltpu.make_async_copy(d_hbm, d_v, in_sem.at[0])
    load_w = pltpu.make_async_copy(w_hbm, w_v, in_sem.at[1])
    load_w.start()
    load_d.start()

    barrier = pltpu.get_barrier_semaphore()
    peers = [{"row_2": other}]
    peers += [{"row_1": turn(x, d, 4)} for d in (1, 2, 3)]
    peers += [{"row_0": turn(y, d, 4)} for d in (1, 2, 3)]
    peers += [{"grp": turn(z, d, 8)} for d in range(1, 8)]
    for peer in peers:
        pl.semaphore_signal(barrier, inc=1, device_id=peer, device_id_type=MESH)

    g = g_ref[...]
    total = jnp.full((8, 128), jnp.sum(g * g), F32)
    load_w.wait()
    w = w_v[...]
    wh = w.astype(BF16)
    wst[0:128] = wh
    wst[128:256] = (w - wh.astype(F32)).astype(BF16)
    load_d.wait()
    pl.semaphore_wait(barrier, len(peers))

    def split(v):
        vh = v.astype(BF16)
        return vh, (v - vh.astype(F32)).astype(BF16)

    def weighted_chunk(j):
        cols = pl.ds(256 * j, 256)
        dh, dl = split(d_v[:, cols])
        both = jnp.dot(wst[...], dh, preferred_element_type=F32)
        acc = both[:128] + both[128:] + jnp.dot(wst[0:128], dl, preferred_element_type=F32)
        dh, dl = split(d_v[cols, :])
        dims = (((1,), (1,)), ((), ()))
        both = lax.dot_general(wst[...], dh, dims, preferred_element_type=F32)
        acc += both[:128] + both[128:]
        acc += lax.dot_general(wst[0:128], dl, dims, preferred_element_type=F32)
        wt[:, cols] = 0.5 * acc

    groups = [peers[0:1], peers[1:4], peers[4:7], peers[7:14]]
    slot = 0
    stats = []
    for n, group in enumerate(groups):
        stat_s[n] = total
        sent = [c(stat_s.at[n], stat_r.at[slot + i], peer) for i, peer in enumerate(group)]
        weighted_chunk(n)
        for i, copy in enumerate(sent):
            copy.wait_recv()
            total += stat_r[slot + i]
        slot += len(group)
        stats += sent

    clip = jnp.minimum(1.0, threshold * lax.rsqrt(total[0:1, 0:1]))
    t = (clip * g_ref[...] + wt[...]).astype(BF16)
    t_ref[...] = t
    own = pl.ds(pl.multiple_of(128 * k, 128), 128)
    xd[own, 0:1024] = t
    xd[own, 1024:1536] = t[:, 0:512]
    pair = c(xd.at[own], xd.at[own], {"row_2": other})
    pair.wait_recv()

    for i in range(4):
        at = pl.multiple_of(128 * (2 * i + k), 128)
        part = lax.dot_general(
            xd[:, pl.ds(at, 128)], xd[:, pl.ds(at, WIN)], (((0,), (0,)), ((), ())),
            preferred_element_type=F32)
        pa[i] = part[:64]
        pb[i] = part[64:]

    sum_a = RingSum(c, "row_1", x, pa, ta, ua, ra, 32)
    sum_b = RingSum(c, "row_0", y, pb, tb, ub, rb, 32)
    sum_a.first()
    sum_b.first()
    sum_a.second()
    sum_b.second()
    va = sum_a.third()
    for j in range(4):
        qa[j] = va[16 * j:16 * j + 16]
    sum_a2 = RingSum(c, "row_0", y, qa, ta2, ua2, ra2, 8)
    sum_a2.first()
    vb = sum_b.third()
    for j in range(4):
        qb[j] = vb[16 * j:16 * j + 16]
    sum_b2 = RingSum(c, "row_1", x, qb, tb2, ub2, rb2, 8)
    sum_b2.first()
    sum_a2.second()
    sum_b2.second()

    fa[k, x, y] = sum_a2.third()
    spread_a = RingSpread(c, "row_0", y, fa.at[k, x], 8)
    spread_a.first()
    fb[k, y, x] = sum_b2.third()
    spread_b = RingSpread(c, "row_1", x, fb.at[k, y], 8)
    spread_b.first()
    spread_a.second()
    spread_b.second()
    spread_a.near()
    spread_a.last()

    far_a = RingSpread(c, "row_1", x, fa.at[k], 2)
    far_a.first()
    shared = [c(fa.at[k, x], fa.at[k, x], {"row_2": other})]
    spread_b.near()
    spread_b.last()
    far_b = RingSpread(c, "row_0", y, fb.at[k], 2)
    far_b.first()
    shared += [c(fb.at[k, y], fb.at[k, y], {"row_2": other})]
    far_a.second()
    far_b.second()
    far_a.near()
    for d in (1, 3):
        p = turn(x, d, 4)
        shared += [c(fa.at[k, p], fa.at[k, p], {"row_2": other})]
    far_b.near()
    for d in (1, 3):
        p = turn(y, d, 4)
        shared += [c(fb.at[k, p], fb.at[k, p], {"row_2": other})]
    far_a.last()
    p = turn(x, 2, 4)
    shared += [c(fa.at[k, p], fa.at[k, p], {"row_2": other})]
    far_b.last()
    p = turn(y, 2, 4)
    shared += [c(fb.at[k, p], fb.at[k, p], {"row_2": other})]
    for copy in shared:
        copy.wait_recv()

    for core in range(2):
        for i in range(4):
            b = 2 * i + core
            for half, f in ((0, fa), (1, fb)):
                rows = pl.ds(128 * b + 64 * half, 64)
                for j in range(5):
                    m = (b + j) % 8
                    gram_ref[rows, 128 * m:128 * m + 128] = (
                        f[core, i, :, :, 128 * j:128 * j + 128].reshape(64, 128))
            for j in range(1, 4):
                m = (b + j) % 8
                gram_ref[128 * m:128 * m + 128, 128 * b:128 * b + 128] = (
                    gram_ref[128 * b:128 * b + 128, 128 * m:128 * m + 128].T)

    for copy in stats + [pair] + shared:
        copy.wait_send()
    for ring in (sum_a, sum_b, sum_a2, sum_b2, spread_a, spread_b, far_a, far_b):
        ring.drain()


def gram_of(gradient, weight, dual, threshold):
    vmem = lambda *s: pltpu.VMEM(s, F32)
    n_copies = 14 + 1 + 8 * 6 + 8
    return pl.pallas_call(
        lambda *refs: gram_kernel(threshold, *refs),
        out_shape=(jax.ShapeDtypeStruct((128, 1024), BF16),
                   jax.ShapeDtypeStruct((1024, 1024), F32)),
        in_specs=[pl.BlockSpec(memory_space=pltpu.VMEM), pl.BlockSpec(memory_space=pl.ANY),
                  pl.BlockSpec(memory_space=pl.ANY)],
        out_specs=[pl.BlockSpec(memory_space=pltpu.VMEM)] * 2,
        scratch_shapes=[
            vmem(128, 1024), vmem(1024, 1024), pltpu.VMEM((256, 1024), BF16), vmem(128, 1024),
            vmem(4, 8, 128), vmem(14, 8, 128), pltpu.VMEM((256, 1536), BF16),
            vmem(4, 64, WIN), vmem(4, 64, WIN), vmem(2, 32, WIN), vmem(2, 32, WIN),
            vmem(2, 32, WIN), vmem(2, 32, WIN), vmem(2, 64, WIN), vmem(2, 64, WIN),
            vmem(4, 16, WIN), vmem(4, 16, WIN), vmem(2, 8, WIN), vmem(2, 8, WIN),
            vmem(2, 8, WIN), vmem(2, 8, WIN), vmem(2, 16, WIN), vmem(2, 16, WIN),
            vmem(2, 4, 4, 16, WIN), vmem(2, 4, 4, 16, WIN),
            pltpu.SemaphoreType.DMA((2,)), pltpu.SemaphoreType.DMA((n_copies,)),
            pltpu.SemaphoreType.DMA((n_copies,)),
        ],
        compiler_params=pltpu.CompilerParams(
            collective_id=0, has_side_effects=True, vmem_limit_bytes=60000 * 1024),
        name="gram",
    )(gradient, weight, dual)


def split_up(shard, dim, size):
    before, after = (shard.shape[:dim], shard.shape[dim + 1 :])
    return jnp.moveaxis(shard.reshape(*before, size, -1, *after), dim, 0)


def sent_and_summed(shard, axis, dim):
    blocks = split_up(shard, dim, lax.axis_size(axis))
    arrived = lax.all_to_all(blocks, axis, split_axis=0, concat_axis=0, tiled=True)
    return arrived.astype(jnp.float32).sum(axis=0)


def summed_rows(shard, axes, dim):
    far, near = axes
    own = sent_and_summed(split_up(shard, dim, lax.axis_size(far)), near, dim + 1)
    return jnp.sum(
        lax.all_to_all(own.astype(jnp.bfloat16), far, 0, 0, tiled=True).astype(jnp.float32), axis=0
    )


def bdot(u, v):
    return jnp.dot(u.astype(BF16), v.astype(BF16), preferred_element_type=F32)


def local(gradient, weight, dual):
    weight_rows = weight[0]
    dual_full = dual[0]
    local_rows, col_count = gradient.shape[1:]
    row_devices = lax.axis_size(ROW)
    group_devices = lax.axis_size("grp")
    share_rows = col_count // row_devices
    threshold = 0.5 * math.sqrt(local_rows * row_devices * col_count * group_devices)
    target, gram = gram_of(gradient[0], weight_rows, dual_full, threshold)
    scale = 1.0 / (jnp.trace(gram) + epsilon)
    gram = gram * scale
    root = jnp.sqrt(scale)
    rows = None
    for step in range(3):
        gh = gram.astype(BF16)
        poly = (coef_b * gram + coef_c * bdot(gh, gh)).astype(BF16)
        if rows is None:
            rows = root * (coef_a * target.astype(F32) + bdot(target, poly))
        else:
            rows = coef_a * rows + bdot(rows, poly)
        if step < 2:
            half = coef_a * gram + bdot(poly, gh)
            gram = coef_a * half + bdot(half, poly)

    def by_gram(v):
        v = bdot(coef_a * v + bdot(v, poly), gh)
        return coef_a * v + bdot(v, poly)

    once = by_gram(rows)
    rows = coef_a * rows + coef_b * once + coef_c * by_gram(once)
    iterate = rows.astype(BF16)
    width_root = math.sqrt(col_count)
    update = width_root * iterate.astype(F32)
    wb = weight_rows.astype(BF16)
    tn = (((0,), (0,)), ((), ()))
    cross = lax.dot_general(wb, iterate, tn, preferred_element_type=F32)
    cross += lax.dot_general(iterate, wb, tn, preferred_element_type=F32)
    summed = summed_rows(cross.astype(BF16), (("row_0", "row_1"), "row_2"), 0)
    own_rows = lax.dynamic_slice_in_dim(dual_full, lax.axis_index(ROW) * share_rows, share_rows, 0)
    dual_next = own_rows - width_root * 0.5 * summed
    return (update[None], dual_next[None])


def solution(mesh):
    torus = Mesh(
        mesh.devices.reshape(mesh.shape["grp"], 4, 4, 2), ("grp", "row_0", "row_1", "row_2")
    )
    in_specs = (P("grp", ROW, None), P("grp", ROW, None), P("grp", None, None))
    out_specs = (P("grp", ROW, None), P("grp", ROW, None))
    return jax.shard_map(local, mesh=torus, in_specs=in_specs, out_specs=out_specs, check_vma=False)
```

```python
import math

import jax
import jax.numpy as jnp
from jax import lax
from jax.experimental import pallas as pl
from jax.experimental.pallas import tpu as pltpu
from jax.sharding import Mesh
from jax.sharding import PartitionSpec as P

ROW = ("row_0", "row_1", "row_2")
MESH = pl.DeviceIdType.MESH
coef_a = 3.4445
coef_b = -4.775
coef_c = 2.0315
epsilon = 1e-06
WIN = 640
STEP_AT = (1, 6, 10, 14, 18, 22, 27)
F32 = jnp.float32
BF16 = jnp.bfloat16


class Copies:
    def __init__(self, send, recv):
        self.send, self.recv, self.n = send, recv, 0

    def __call__(self, src, dst, where):
        i = self.n
        self.n += 1
        copy = pltpu.make_async_remote_copy(
            src_ref=src, dst_ref=dst, send_sem=self.send.at[i], recv_sem=self.recv.at[i],
            device_id=where, device_id_type=MESH,
        )
        copy.start()
        return copy


def turn(p, d, n):
    return lax.rem(p + d, n)


class RingSum:
    def __init__(self, copies, axis, p, part, bufs, lo, hi):
        self.c, self.axis, self.p, self.part = copies, axis, p, part
        self.t, self.u, self.r = bufs
        self.lo, self.hi = lo, hi

    def first(self):
        c, p, part, t, r = self.c, self.p, self.part, self.t, self.r
        right, left, far = turn(p, 1, 4), turn(p, 3, 4), turn(p, 2, 4)
        to_r, to_l = {self.axis: right}, {self.axis: left}
        lo, hi = self.lo, self.hi
        self.a = c(part.at[(far, *lo)], t.at[0], to_r)
        self.b = c(part.at[(far, *hi)], t.at[1], to_l)
        self.e = c(part.at[(right, *hi)], r.at[(0, *hi)], to_r)
        self.f = c(part.at[(left, *lo)], r.at[(1, *lo)], to_l)

    def second(self):
        c, p, part, t, u, r = self.c, self.p, self.part, self.t, self.u, self.r
        right, left = turn(p, 1, 4), turn(p, 3, 4)
        lo, hi = self.lo, self.hi
        self.a.wait_recv()
        u[0] = (part[(right, *lo)].astype(F32) + t[0].astype(F32)).astype(u.dtype)
        self.g = c(u.at[0], r.at[(0, *lo)], {self.axis: right})
        self.b.wait_recv()
        u[1] = (part[(left, *hi)].astype(F32) + t[1].astype(F32)).astype(u.dtype)
        self.i = c(u.at[1], r.at[(1, *hi)], {self.axis: left})

    def third(self):
        for copy in (self.e, self.f, self.g, self.i):
            copy.wait_recv()
        return self.part[self.p].astype(F32) + self.r[0].astype(F32) + self.r[1].astype(F32)

    def drain(self):
        for copy in (self.a, self.b, self.e, self.f, self.g, self.i):
            copy.wait_send()


class RingSpread:
    def __init__(self, copies, axis, p, at, lo, hi):
        self.c, self.axis, self.p = copies, axis, p
        self.lo = lambda i: at(i, lo)
        self.hi = lambda i: at(i, hi)

    def first(self):
        c, p, lo, hi = self.c, self.p, self.lo, self.hi
        to_r, to_l = {self.axis: turn(p, 1, 4)}, {self.axis: turn(p, 3, 4)}
        self.a = c(lo(p), lo(p), to_r)
        self.b = c(hi(p), hi(p), to_l)
        self.e = c(hi(p), hi(p), to_r)
        self.f = c(lo(p), lo(p), to_l)

    def second(self):
        c, p, lo, hi = self.c, self.p, self.lo, self.hi
        right, left = turn(p, 1, 4), turn(p, 3, 4)
        self.a.wait_recv()
        self.g = c(lo(left), lo(left), {self.axis: right})
        self.b.wait_recv()
        self.i = c(hi(right), hi(right), {self.axis: left})

    def near(self):
        self.e.wait_recv()
        self.f.wait_recv()

    def last(self):
        self.g.wait_recv()
        self.i.wait_recv()

    def drain(self):
        for copy in (self.a, self.b, self.e, self.f, self.g, self.i):
            copy.wait_send()


def everywhere(c, x, y, k, parts_a, parts_b, bufs, cut1, cut2, near_at, far_at, order):
    other = {"row_2": 1 - k}
    ba, bb, qa, qb, ba2, bb2 = bufs
    dtype = qa.dtype
    near_a, near_b = near_at
    far_a_at, far_b_at = far_at
    sum_a = RingSum(c, "row_1", x, parts_a, ba, *cut1)
    sum_b = RingSum(c, "row_0", y, parts_b, bb, *cut1)
    sum_a.first()
    sum_b.first()
    yield
    sum_a.second()
    sum_b.second()
    yield
    va = sum_a.third().astype(dtype)
    for j in range(4):
        qa[j] = va[16 * j:16 * j + 16]
    sum_a2 = RingSum(c, "row_0", y, qa, ba2, *cut2)
    sum_a2.first()
    vb = sum_b.third().astype(dtype)
    for j in range(4):
        qb[j] = vb[16 * j:16 * j + 16]
    sum_b2 = RingSum(c, "row_1", x, qb, bb2, *cut2)
    sum_b2.first()
    yield
    sum_a2.second()
    sum_b2.second()
    yield
    near_a(y, ())[...] = sum_a2.third().astype(dtype)
    spread_a = RingSpread(c, "row_0", y, near_a, *cut2)
    spread_a.first()
    near_b(x, ())[...] = sum_b2.third().astype(dtype)
    spread_b = RingSpread(c, "row_1", x, near_b, *cut2)
    spread_b.first()
    yield
    spread_a.second()
    spread_b.second()
    yield
    spread_a.near()
    spread_a.last()
    halves = (pl.ds(0, 2), pl.ds(2, 2))
    far_a = RingSpread(c, "row_1", x, far_a_at, *halves)
    far_a.first()
    every = slice(None)
    pair = lambda ref: c(ref, ref, other)
    shared = [pair(far_a_at(x, every))]
    spread_b.near()
    spread_b.last()
    far_b = RingSpread(c, "row_0", y, far_b_at, *halves)
    far_b.first()
    shared += [pair(far_b_at(y, every))]
    yield
    far_a.second()
    far_b.second()
    yield
    far_a.near()
    shared += [pair(far_a_at(turn(x, d, 4), every)) for d in (1, 3)]
    far_b.near()
    shared += [pair(far_b_at(turn(y, d, 4), every)) for d in (1, 3)]
    yield
    far_a.last()
    shared += [pair(far_a_at(turn(x, 2, 4), every))]
    far_b.last()
    shared += [pair(far_b_at(turn(y, 2, 4), every))]
    yield
    for copy in shared:
        copy.wait_recv()
    order.append(shared)
    order.append((sum_a, sum_b, sum_a2, sum_b2, spread_a, spread_b, far_a, far_b))


def kernel(threshold, g_hbm, w_hbm, d_hbm, x_out, dual_out,
           g_ref, w_v, d_v, wst, wt, wt2, g2, stat_s, stat_r, xd, wd, cp, pa, pb, fin, gf, gh, p0, p1, p2, uf, ub,
           ca, cb, cfin, bufs_g, bufs_c, in_sem, send, recv):
    z = lax.axis_index("grp")
    y = lax.axis_index("row_0")
    x = lax.axis_index("row_1")
    k = lax.axis_index("row_2")
    other = 1 - k
    c = Copies(send, recv)
    load_d = pltpu.make_async_copy(d_hbm, d_v, in_sem.at[0])
    load_w = pltpu.make_async_copy(w_hbm, w_v, in_sem.at[1])
    load_g = pltpu.make_async_copy(g_hbm, g_ref, in_sem.at[2])
    load_g.start()
    load_w.start()
    load_d.start()

    barrier = pltpu.get_barrier_semaphore()
    partner = {"row_2": other}
    plane = [{"row_0": turn(y, e, 4), "row_1": turn(x, d, 4), "row_2": turn(k, f, 2)}
             for e in range(4) for d in range(4) for f in range(2) if (e, d, f) != (0, 0, 0)]
    line = [{"grp": turn(z, d, 8)} for d in range(1, 8)]
    for peer in plane + line:
        pl.semaphore_signal(barrier, inc=1, device_id=peer, device_id_type=MESH)

    load_g.wait()
    g = g_ref[...]
    total = jnp.full((1, 128), jnp.sum(g * g), F32)
    stat_s[0] = total
    own = pl.ds(pl.multiple_of(128 * k, 128), 128)
    theirs = pl.ds(pl.multiple_of(128 * other, 128), 128)
    pl.semaphore_wait(barrier, len(plane) + len(line))
    stats = [c(stat_s.at[0], stat_r.at[i], peer) for i, peer in enumerate(plane)]
    pairs = [c(g_ref, g2, partner)]
    load_w.wait()
    w = w_v[...]
    wh = w.astype(BF16)
    wst[0:128] = wh
    wst[128:256] = (w - wh.astype(F32)).astype(BF16)
    wd[own] = wh
    pairs.append(c(wd.at[own], wd.at[own], partner))
    load_d.wait()

    def split(v):
        vh = v.astype(BF16)
        return vh, (v - vh.astype(F32)).astype(BF16)

    def weighted_chunk(j):
        cols = pl.ds(256 * j, 256)
        dh, dl = split(d_v[:, cols])
        both = jnp.dot(wst[...], dh, preferred_element_type=F32)
        acc = both[:128] + both[128:] + jnp.dot(wst[0:128], dl, preferred_element_type=F32)
        dh, dl = split(d_v[cols, :])
        dims = (((1,), (1,)), ((), ()))
        both = lax.dot_general(wst[...], dh, dims, preferred_element_type=F32)
        acc += both[:128] + both[128:]
        acc += lax.dot_general(wst[0:128], dl, dims, preferred_element_type=F32)
        wt[:, cols] = 0.5 * acc

    def half_weighted(m):
        for n in (2 * m, 2 * m + 1):
            weighted_chunk(n)
        cols = pl.ds(512 * m, 512)
        pairs.append(c(wt.at[:, cols], wt2.at[:, cols], partner))

    half_weighted(0)
    for i, copy in enumerate(stats):
        copy.wait_recv()
        total += stat_r[i]
    stat_s[1] = total
    lines = [c(stat_s.at[1], stat_r.at[31 + i], peer) for i, peer in enumerate(line)]
    half_weighted(1)
    for copy in pairs:
        copy.wait_recv()
    for i, copy in enumerate(lines):
        copy.wait_recv()
        total += stat_r[31 + i]

    clip = jnp.minimum(1.0, threshold * lax.rsqrt(total[0:1, 0:1]))
    for rows, ga, wa in ((own, g_ref, wt), (theirs, g2, wt2)):
        t = (clip * ga[...] + wa[...]).astype(BF16)
        xd[rows, 0:1024] = t
        xd[rows, 1024:1536] = t[:, 0:512]

    tn = (((0,), (0,)), ((), ()))
    for i in range(4):
        at = pl.multiple_of(128 * (2 * i + k), 128)
        part = lax.dot_general(
            xd[:, pl.ds(at, 128)], xd[:, pl.ds(at, WIN)], tn, preferred_element_type=F32)
        pa[i] = part[:64]
        pb[i] = part[64:]

    ended = []
    rows8 = ((pl.ds(0, 8),), (pl.ds(8, 8),))
    rows32 = ((pl.ds(0, 32),), (pl.ds(32, 32),))
    gram_steps = everywhere(
        c, x, y, k, pa, pb, bufs_g, rows32, rows8,
        (lambda j, h: fin.at[(x, k, 0, j, *h)], lambda j, h: fin.at[(y, k, 1, j, *h)]),
        (lambda i, h: fin.at[i, k, 0, h], lambda i, h: fin.at[i, k, 1, h]), ended)
    next(gram_steps)
    next(gram_steps)
    for b in range(8):
        part = lax.dot_general(
            wd[:, 128 * b:128 * b + 128], xd[:, 0:1024], tn, preferred_element_type=F32)
        cp[b] = part.astype(BF16).reshape(2, 2, 2, 16, 1024)
    for e in range(4):
        for d in range(4):
            ca[d, 16 * e:16 * e + 16] = cp[2 * e + d // 2, d % 2, k, 0]
            cb[e, 16 * d:16 * d + 16] = cp[2 * e + d // 2, d % 2, k, 1]
    for _ in range(6):
        next(gram_steps)

    cols512 = ((slice(None), pl.ds(0, 512)), (slice(None), pl.ds(512, 512)))
    steps = everywhere(
        c, x, y, k, ca, cb, bufs_c, rows32, cols512,
        (lambda j, h: cfin.at[(j, x, k, 0, *h)], lambda j, h: cfin.at[(y, j, k, 1, *h)]),
        (lambda i, h: cfin.at[h, i, k, 0], lambda i, h: cfin.at[i, h, k, 1]), ended)
    next(steps)
    for _ in gram_steps:
        pass

    trace = jnp.zeros((1, 1), F32)
    eye = (lax.broadcasted_iota(jnp.int32, (128, 128), 0)
           == lax.broadcasted_iota(jnp.int32, (128, 128), 1))
    for b in range(8):
        i, core = b // 2, b % 2
        for j in range(5):
            m = (b + j) % 8
            block = fin[i, core, :, :, :, 128 * j:128 * j + 128].reshape(128, 128)
            rows, cols = pl.ds(128 * b, 128), pl.ds(128 * m, 128)
            gf[rows, cols] = block
            gh[rows, cols] = block.astype(BF16)
            if j == 0:
                trace += jnp.sum(jnp.where(eye, block, 0.0), keepdims=True)
            if 0 < j < 4:
                block = block.T
                gf[cols, rows] = block
                gh[cols, rows] = block.astype(BF16)
    scale = 1.0 / (trace + epsilon)
    root = jnp.sqrt(scale)

    def dot(u, v):
        return jnp.dot(u, v, preferred_element_type=F32)

    TILE = 256
    tiles = [pl.ds(TILE * n, TILE) for n in range(1024 // TILE)]
    done = [0]

    def advance():
        done[0] += 1
        if done[0] in STEP_AT:
            next(steps, None)

    for step, p in enumerate((p0, p1, p2)):
        s = scale if step == 0 else 1.0
        for n in tiles:
            p[:, n] = ((coef_b * s) * gf[:, n]
                       + (coef_c * s * s) * dot(gh[...], gh[:, n])).astype(BF16)
            advance()
        if step < 2:
            for n in tiles:
                u = coef_a * gf[:, n] + dot(p[...], gh[:, n])
                uf[:, n] = u
                ub[:, n] = u.astype(BF16)
                advance()
            for n in tiles:
                v = s * (coef_a * uf[:, n] + dot(ub[...], p[:, n]))
                gf[:, n] = v
                gh[:, n] = v.astype(BF16)
                advance()

    mine = cfin[y, x, k].reshape(32, 1024)
    share = 8 * y + 2 * x + k
    unit = (lax.broadcasted_iota(jnp.int32, (32, 1024), 0) + 32 * share
            == lax.broadcasted_iota(jnp.int32, (32, 1024), 1))
    low = jnp.concatenate([xd[own, 0:1024], mine, unit.astype(F32).astype(BF16)], axis=0)
    v = coef_a * low.astype(F32) + dot(low, p0[...])
    v = coef_a * v + dot(v.astype(BF16), p1[...])
    v = coef_a * v + dot(v.astype(BF16), p2[...])

    def by_gram(v):
        v = dot((coef_a * v + dot(v.astype(BF16), p2[...])).astype(BF16), gh[...])
        return coef_a * v + dot(v.astype(BF16), p2[...])

    next(steps)
    once = by_gram(v)
    next(steps)
    v = coef_a * v + coef_b * once + coef_c * by_gram(once)
    for _ in steps:
        pass
    x_out[...] = (root * v[0:128]).astype(BF16)
    cross = v[128:160] + lax.dot_general(
        v[160:192].astype(BF16), cfin[...].reshape(1024, 1024), (((1,), (1,)), ((), ())),
        preferred_element_type=F32)
    dual_out[...] = d_v[pl.ds(pl.multiple_of(32 * share, 32), 32), :] - (16.0 * root) * cross

    for copy in stats + lines + pairs:
        copy.wait_send()
    for group in ended:
        for item in group:
            item.drain() if hasattr(item, "drain") else item.wait_send()


def step_of(gradient, weight, dual, threshold):
    vmem = lambda *s: pltpu.VMEM(s, F32)
    half = lambda *s: pltpu.VMEM(s, BF16)

    def bufs(kind, width, cut2):
        first = [kind(2, 32, width), kind(2, 32, width), kind(2, 64, width)]
        second = [kind(2, *cut2), kind(2, *cut2), kind(2, 16, width)]
        return [first, first, kind(4, 16, width), kind(4, 16, width), second, second]

    n_copies = 38 + 4 + 2 * (8 * 6 + 8)
    return pl.pallas_call(
        lambda *refs: kernel(threshold, *refs),
        out_shape=(jax.ShapeDtypeStruct((128, 1024), BF16),
                   jax.ShapeDtypeStruct((32, 1024), F32)),
        in_specs=[pl.BlockSpec(memory_space=pltpu.HBM)] * 3,
        out_specs=[pl.BlockSpec(memory_space=pltpu.VMEM)] * 2,
        scratch_shapes=[
            vmem(128, 1024), vmem(128, 1024), vmem(1024, 1024), half(256, 1024), vmem(128, 1024),
            vmem(128, 1024), vmem(128, 1024), vmem(2, 1, 128), vmem(38, 1, 128), half(256, 1536), half(256, 1024),
            half(8, 2, 2, 2, 16, 1024),
            vmem(4, 64, WIN), vmem(4, 64, WIN), vmem(4, 2, 2, 4, 16, WIN),
            vmem(1024, 1024), half(1024, 1024), half(1024, 1024), half(1024, 1024),
            half(1024, 1024), vmem(1024, 1024), half(1024, 1024),
            half(4, 64, 1024), half(4, 64, 1024), half(4, 4, 2, 2, 16, 1024),
            bufs(vmem, WIN, (8, WIN)), bufs(half, 1024, (16, 512)),
            pltpu.SemaphoreType.DMA((3,)), pltpu.SemaphoreType.DMA((n_copies,)),
            pltpu.SemaphoreType.DMA((n_copies,)),
        ],
        compiler_params=pltpu.CompilerParams(
            collective_id=0, has_side_effects=True, vmem_limit_bytes=59000 * 1024),
        name="step",
    )(gradient, weight, dual)


def local(gradient, weight, dual):
    local_rows, col_count = gradient.shape[1:]
    threshold = 0.5 * math.sqrt(
        local_rows * lax.axis_size(ROW) * col_count * lax.axis_size("grp"))
    iterate, dual_next = step_of(gradient[0], weight[0], dual[0], threshold)
    update = math.sqrt(col_count) * iterate.astype(F32)
    return (update[None], dual_next[None])


def solution(mesh):
    torus = Mesh(
        mesh.devices.reshape(mesh.shape["grp"], 4, 4, 2), ("grp", "row_0", "row_1", "row_2")
    )
    in_specs = (P("grp", ROW, None), P("grp", ROW, None), P("grp", None, None))
    out_specs = (P("grp", ROW, None), P("grp", ROW, None))
    return jax.shard_map(local, mesh=torus, in_specs=in_specs, out_specs=out_specs, check_vma=False)
```

```python
import math

import jax
import jax.numpy as jnp
from jax import lax
from jax.experimental import pallas as pl
from jax.experimental.pallas import tpu as pltpu
from jax.sharding import Mesh
from jax.sharding import PartitionSpec as P

ROW = ("row_0", "row_1", "row_2")
MESH = pl.DeviceIdType.MESH
coef_a = 3.4445
coef_b = -4.775
coef_c = 2.0315
epsilon = 1e-06
WIN = 640
STEPS = {8: (1,), 15: (1, 2), 22: (2,)}
F32 = jnp.float32
BF16 = jnp.bfloat16


class Copies:
    def __init__(self, send, recv):
        self.send, self.recv, self.n = send, recv, 0

    def __call__(self, src, dst, where):
        i = self.n
        self.n += 1
        copy = pltpu.make_async_remote_copy(
            src_ref=src, dst_ref=dst, send_sem=self.send.at[i], recv_sem=self.recv.at[i],
            device_id=where, device_id_type=MESH,
        )
        copy.start()
        return copy


def turn(p, d, n):
    return lax.rem(p + d, n)


class Sum:
    def __init__(self, copies, axis, p, part, arrived):
        self.p, self.part, self.arrived = p, part, arrived
        self.sent = [copies(part.at[turn(p, d, 4)], arrived.at[d - 1], {axis: turn(p, d, 4)})
                     for d in (2, 1, 3)]

    def total(self):
        for copy in self.sent:
            copy.wait_recv()
        out = self.part[self.p].astype(F32)
        for d in range(3):
            out += self.arrived[d].astype(F32)
        return out


class Spread:
    def __init__(self, copies, axis, p, at):
        self.sent = [copies(at(p), at(p), {axis: turn(p, d, 4)}) for d in (2, 1, 3)]
        self.came = [at(turn(p, 4 - d, 4)) for d in (2, 1, 3)]

    def each(self):
        for copy, ref in ((self.sent[i], self.came[i]) for i in (1, 2, 0)):
            copy.wait_recv()
            yield ref


def reduce_steps(c, x, y, parts_a, parts_b, bufs, put_a, put_b, sent):
    ra, rb, qa, qb, ra2, rb2 = bufs
    dtype = qa.dtype
    sum_a = Sum(c, "row_1", x, parts_a, ra)
    sum_b = Sum(c, "row_0", y, parts_b, rb)
    yield
    va = sum_a.total().astype(dtype)
    for j in range(4):
        qa[j] = va[16 * j:16 * j + 16]
    sum_a2 = Sum(c, "row_0", y, qa, ra2)
    vb = sum_b.total().astype(dtype)
    for j in range(4):
        qb[j] = vb[16 * j:16 * j + 16]
    sum_b2 = Sum(c, "row_1", x, qb, rb2)
    yield
    put_a(sum_a2.total())
    put_b(sum_b2.total())
    for phase in (sum_a, sum_b, sum_a2, sum_b2):
        sent += phase.sent


def gather_steps(c, x, y, k, near_at, far_at, sent):
    near_a, near_b = near_at
    far_a, far_b = far_at
    shared = []

    def pair(ref):
        shared.append(c(ref, ref, {"row_2": 1 - k}))

    na = Spread(c, "row_0", y, near_a)
    nb = Spread(c, "row_1", x, near_b)
    yield
    for _ in na.each():
        pass
    fa = Spread(c, "row_1", x, far_a)
    for _ in nb.each():
        pass
    fb = Spread(c, "row_0", y, far_b)
    pair(far_a(x))
    pair(far_b(y))
    yield
    for refs in zip(fa.each(), fb.each()):
        for ref in refs:
            pair(ref)
    yield
    for copy in shared:
        copy.wait_recv()
    for phase in (na, nb, fa, fb):
        sent += phase.sent
    sent += shared


def kernel(threshold, g_hbm, w_hbm, d_hbm, x_out, dual_out,
           g_ref, w_v, d_v, wst, wt, wt2, g2, stat_s, stat_r, xd, wd, cp, pa, pb, fin, fil, gf, gh, gl, p0, p1, p2, uf, ub,
           ca, cb, cfin, bufs_g, bufs_c, in_sem, send, recv):
    z = lax.axis_index("grp")
    y = lax.axis_index("row_0")
    x = lax.axis_index("row_1")
    k = lax.axis_index("row_2")
    other = 1 - k
    c = Copies(send, recv)
    load_d = pltpu.make_async_copy(d_hbm, d_v, in_sem.at[0])
    load_w = pltpu.make_async_copy(w_hbm, w_v, in_sem.at[1])
    load_g = pltpu.make_async_copy(g_hbm, g_ref, in_sem.at[2])
    load_g.start()
    load_w.start()
    load_d.start()

    barrier = pltpu.get_barrier_semaphore()
    partner = {"row_2": other}
    plane = [{"row_0": turn(y, e, 4), "row_1": turn(x, d, 4), "row_2": turn(k, f, 2)}
             for e in range(4) for d in range(4) for f in range(2) if (e, d, f) != (0, 0, 0)]
    line = [{"grp": turn(z, d, 8)} for d in range(1, 8)]
    for peer in plane + line:
        pl.semaphore_signal(barrier, inc=1, device_id=peer, device_id_type=MESH)

    load_g.wait()
    g = g_ref[...]
    total = jnp.full((1, 128), jnp.sum(g * g), F32)
    stat_s[0] = total
    own = pl.ds(pl.multiple_of(128 * k, 128), 128)
    theirs = pl.ds(pl.multiple_of(128 * other, 128), 128)
    pl.semaphore_wait(barrier, len(plane) + len(line))
    stats = [c(stat_s.at[0], stat_r.at[i], peer) for i, peer in enumerate(plane)]
    pairs = [c(g_ref, g2, partner)]
    load_w.wait()
    w = w_v[...]
    wh = w.astype(BF16)
    wst[0:128] = wh
    wst[128:256] = (w - wh.astype(F32)).astype(BF16)
    wd[own] = wh
    pairs.append(c(wd.at[own], wd.at[own], partner))
    load_d.wait()

    def split(v):
        vh = v.astype(BF16)
        return vh, (v - vh.astype(F32)).astype(BF16)

    def weighted_chunk(j):
        cols = pl.ds(256 * j, 256)
        dh, dl = split(d_v[:, cols])
        both = jnp.dot(wst[...], dh, preferred_element_type=F32)
        acc = both[:128] + both[128:] + jnp.dot(wst[0:128], dl, preferred_element_type=F32)
        dh, dl = split(d_v[cols, :])
        dims = (((1,), (1,)), ((), ()))
        both = lax.dot_general(wst[...], dh, dims, preferred_element_type=F32)
        acc += both[:128] + both[128:]
        acc += lax.dot_general(wst[0:128], dl, dims, preferred_element_type=F32)
        wt[:, cols] = 0.5 * acc

    def half_weighted(m):
        for n in (2 * m, 2 * m + 1):
            weighted_chunk(n)
        cols = pl.ds(512 * m, 512)
        pairs.append(c(wt.at[:, cols], wt2.at[:, cols], partner))

    half_weighted(0)
    for i, copy in enumerate(stats):
        copy.wait_recv()
        total += stat_r[i]
    stat_s[1] = total
    lines = [c(stat_s.at[1], stat_r.at[31 + i], peer) for i, peer in enumerate(line)]
    half_weighted(1)
    for copy in pairs:
        copy.wait_recv()
    for i, copy in enumerate(lines):
        copy.wait_recv()
        total += stat_r[31 + i]

    clip = jnp.minimum(1.0, threshold * lax.rsqrt(total[0:1, 0:1]))
    for rows, ga, wa in ((own, g_ref, wt), (theirs, g2, wt2)):
        t = (clip * ga[...] + wa[...]).astype(BF16)
        xd[rows, 0:1024] = t
        xd[rows, 1024:1536] = t[:, 0:512]

    tn = (((0,), (0,)), ((), ()))
    for i in range(4):
        at = pl.multiple_of(128 * (2 * i + k), 128)
        part = lax.dot_general(
            xd[:, pl.ds(at, 128)], xd[:, pl.ds(at, WIN)], tn, preferred_element_type=F32)
        pa[i] = part[:64]
        pb[i] = part[64:]

    ended = []

    def put_gram(at_hi, at_lo):
        def put(v):
            hi = v.astype(BF16)
            at_hi[...] = hi
            at_lo[...] = (v - hi.astype(F32)).astype(BF16)
        return put

    near = lambda f: (lambda j: f.at[x, k, 0, j], lambda j: f.at[y, k, 1, j])
    far = lambda f: (lambda i: f.at[i, k, 0], lambda i: f.at[i, k, 1])
    gram_steps = reduce_steps(c, x, y, pa, pb, bufs_g,
                              put_gram(near(fin)[0](y), near(fil)[0](y)),
                              put_gram(near(fin)[1](x), near(fil)[1](x)), ended)
    next(gram_steps)
    for b in range(8):
        part = lax.dot_general(
            wd[:, 128 * b:128 * b + 128], xd[:, 0:1024], tn, preferred_element_type=F32)
        cp[b] = part.astype(BF16).reshape(2, 2, 2, 16, 1024)
    for e in range(4):
        for d in range(4):
            ca[d, 16 * e:16 * e + 16] = cp[2 * e + d // 2, d % 2, k, 0]
            cb[e, 16 * d:16 * d + 16] = cp[2 * e + d // 2, d % 2, k, 1]
    for _ in gram_steps:
        pass
    high = gather_steps(c, x, y, k, near(fin), far(fin), ended)
    low = gather_steps(c, x, y, k, near(fil), far(fil), ended)
    next(high)
    next(low)
    next(high)
    next(low)

    def put_at(ref):
        def put(v):
            ref[...] = v.astype(BF16)
        return put

    product_near = (lambda j: cfin.at[j, x, k, 0], lambda j: cfin.at[y, j, k, 1])
    product_far = (lambda i: cfin.at[:, i, k, 0], lambda i: cfin.at[i, :, k, 1])
    reduced = reduce_steps(c, x, y, ca, cb, bufs_c, put_at(product_near[0](y)),
                           put_at(product_near[1](x)), ended)
    gathered = gather_steps(c, x, y, k, product_near, product_far, ended)
    next(reduced)
    for _ in high:
        pass

    trace = jnp.zeros((1, 1), F32)
    eye = (lax.broadcasted_iota(jnp.int32, (128, 128), 0)
           == lax.broadcasted_iota(jnp.int32, (128, 128), 1))
    for b in range(8):
        i, core = b // 2, b % 2
        for j in range(5):
            m = (b + j) % 8
            block = fin[i, core, :, :, :, 128 * j:128 * j + 128].reshape(128, 128)
            rows, cols = pl.ds(128 * b, 128), pl.ds(128 * m, 128)
            gh[rows, cols] = block
            if j == 0:
                trace += jnp.sum(jnp.where(eye, block.astype(F32), 0.0), keepdims=True)
            if 0 < j < 4:
                gh[cols, rows] = block.T
    scale = 1.0 / (trace + epsilon)
    root = jnp.sqrt(scale)

    def dot(u, v):
        return jnp.dot(u, v, preferred_element_type=F32)

    TILE = 256
    tiles = [pl.ds(TILE * n, TILE) for n in range(1024 // TILE)]
    done = [0]

    def advance():
        done[0] += 1
        for steps in STEPS.get(done[0], ()):
            next((low, reduced, gathered)[steps], None)

    def square(p, n, s):
        g = gh[:, n].astype(F32) if p is p0 else gf[:, n]
        p[:, n] = ((coef_b * s) * g + (coef_c * s * s) * dot(gh[...], gh[:, n])).astype(BF16)
        advance()

    def left(p, n):
        g = gh[:, n].astype(F32) if p is p0 else gf[:, n]
        u = coef_a * g + dot(p[...], gh[:, n])
        uf[:, n] = u
        ub[:, n] = u.astype(BF16)
        advance()

    def right(p, n, s):
        v = coef_a * uf[:, n] + dot(ub[...], p[:, n])
        if p is p0:
            v = s * (v + (coef_a * coef_a) * gl[:, n].astype(F32))
        gf[:, n] = v
        gh[:, n] = v.astype(BF16)
        advance()

    for n in tiles:
        square(p0, n, scale)
    for n in tiles:
        left(p0, n)
    for _ in low:
        pass
    for b in range(8):
        i, core = b // 2, b % 2
        for j in range(5):
            m = (b + j) % 8
            block = fil[i, core, :, :, :, 128 * j:128 * j + 128].reshape(128, 128)
            rows, cols = pl.ds(128 * b, 128), pl.ds(128 * m, 128)
            gl[rows, cols] = block
            if 0 < j < 4:
                gl[cols, rows] = block.T
    for n in tiles:
        right(p0, n, scale)
    for n in tiles:
        square(p1, n, 1.0)
    for n in tiles:
        left(p1, n)
    for n in tiles:
        right(p1, n, 1.0)
    for n in tiles:
        square(p2, n, 1.0)

    mine = cfin[y, x, k].reshape(32, 1024)
    share = 8 * y + 2 * x + k
    unit = (lax.broadcasted_iota(jnp.int32, (32, 1024), 0) + 32 * share
            == lax.broadcasted_iota(jnp.int32, (32, 1024), 1))
    stack = jnp.concatenate([xd[own, 0:1024], mine, unit.astype(F32).astype(BF16)], axis=0)
    v = coef_a * stack.astype(F32) + dot(stack, p0[...])
    v = coef_a * v + dot(v.astype(BF16), p1[...])
    v = coef_a * v + dot(v.astype(BF16), p2[...])

    def by_gram(v):
        v = dot((coef_a * v + dot(v.astype(BF16), p2[...])).astype(BF16), gh[...])
        return coef_a * v + dot(v.astype(BF16), p2[...])

    once = by_gram(v)
    next(gathered)
    v = coef_a * v + coef_b * once + coef_c * by_gram(once)
    for _ in gathered:
        pass
    x_out[...] = (root * v[0:128]).astype(BF16)
    cross = v[128:160] + lax.dot_general(
        v[160:192].astype(BF16), cfin[...].reshape(1024, 1024), (((1,), (1,)), ((), ())),
        preferred_element_type=F32)
    dual_out[...] = d_v[pl.ds(pl.multiple_of(32 * share, 32), 32), :] - (16.0 * root) * cross

    for copy in stats + lines + pairs + ended:
        copy.wait_send()


def step_of(gradient, weight, dual, threshold):
    vmem = lambda *s: pltpu.VMEM(s, F32)
    half = lambda *s: pltpu.VMEM(s, BF16)

    def bufs(kind, width):
        first, second = kind(3, 64, width), kind(3, 16, width)
        return [first, first, kind(4, 16, width), kind(4, 16, width), second, second]

    n_copies = 38 + 4 + 12 * 2 + 20 * 3
    return pl.pallas_call(
        lambda *refs: kernel(threshold, *refs),
        out_shape=(jax.ShapeDtypeStruct((128, 1024), BF16),
                   jax.ShapeDtypeStruct((32, 1024), F32)),
        in_specs=[pl.BlockSpec(memory_space=pltpu.HBM)] * 3,
        out_specs=[pl.BlockSpec(memory_space=pltpu.VMEM)] * 2,
        scratch_shapes=[
            vmem(128, 1024), vmem(128, 1024), vmem(1024, 1024), half(256, 1024), vmem(128, 1024),
            vmem(128, 1024), vmem(128, 1024), vmem(2, 1, 128), vmem(38, 1, 128), half(256, 1536), half(256, 1024),
            half(8, 2, 2, 2, 16, 1024),
            vmem(4, 64, WIN), vmem(4, 64, WIN), half(4, 2, 2, 4, 16, WIN), half(4, 2, 2, 4, 16, WIN),
            vmem(1024, 1024), half(1024, 1024), half(1024, 1024), half(1024, 1024), half(1024, 1024),
            half(1024, 1024), vmem(1024, 1024), half(1024, 1024),
            half(4, 64, 1024), half(4, 64, 1024), half(4, 4, 2, 2, 16, 1024),
            bufs(vmem, WIN), bufs(half, 1024),
            pltpu.SemaphoreType.DMA((3,)), pltpu.SemaphoreType.DMA((n_copies,)),
            pltpu.SemaphoreType.DMA((n_copies,)),
        ],
        compiler_params=pltpu.CompilerParams(
            collective_id=0, has_side_effects=True, vmem_limit_bytes=59000 * 1024),
        name="step",
    )(gradient, weight, dual)


def local(gradient, weight, dual):
    local_rows, col_count = gradient.shape[1:]
    threshold = 0.5 * math.sqrt(
        local_rows * lax.axis_size(ROW) * col_count * lax.axis_size("grp"))
    iterate, dual_next = step_of(gradient[0], weight[0], dual[0], threshold)
    update = math.sqrt(col_count) * iterate.astype(F32)
    return (update[None], dual_next[None])


def solution(mesh):
    torus = Mesh(
        mesh.devices.reshape(mesh.shape["grp"], 4, 4, 2), ("grp", "row_0", "row_1", "row_2")
    )
    in_specs = (P("grp", ROW, None), P("grp", ROW, None), P("grp", None, None))
    out_specs = (P("grp", ROW, None), P("grp", ROW, None))
    return jax.shard_map(local, mesh=torus, in_specs=in_specs, out_specs=out_specs, check_vma=False)
```

```python
import math

import jax
import jax.numpy as jnp
from jax import lax
from jax.experimental import pallas as pl
from jax.experimental.pallas import tpu as pltpu
from jax.sharding import Mesh
from jax.sharding import PartitionSpec as P

ROW = ("row_0", "row_1", "row_2")
MESH = pl.DeviceIdType.MESH
coef_a = 3.4445
coef_b = -4.775
coef_c = 2.0315
epsilon = 1e-06
WIN = 640
STEPS = {1: (1, 2), 7: (2,), 21: (2,)}
F32 = jnp.float32
BF16 = jnp.bfloat16


class Copies:
    def __init__(self, send, recv):
        self.send, self.recv, self.n = send, recv, 0

    def __call__(self, src, dst, where):
        i = self.n
        self.n += 1
        copy = pltpu.make_async_remote_copy(
            src_ref=src, dst_ref=dst, send_sem=self.send.at[i], recv_sem=self.recv.at[i],
            device_id=where, device_id_type=MESH,
        )
        copy.start()
        return copy


def turn(p, d, n):
    return lax.rem(p + d, n)


class Sum:
    def __init__(self, copies, axis, p, part, arrived):
        self.p, self.part, self.arrived = p, part, arrived
        self.sent = [copies(part.at[turn(p, d, 4)], arrived.at[d - 1], {axis: turn(p, d, 4)})
                     for d in (2, 1, 3)]

    def total(self):
        for copy in self.sent:
            copy.wait_recv()
        out = self.part[self.p].astype(F32)
        for d in range(3):
            out += self.arrived[d].astype(F32)
        return out


class Spread:
    def __init__(self, copies, axis, p, at):
        self.sent = [copies(at(p), at(p), {axis: turn(p, d, 4)}) for d in (2, 1, 3)]
        self.came = [at(turn(p, 4 - d, 4)) for d in (2, 1, 3)]

    def each(self):
        for copy, ref in ((self.sent[i], self.came[i]) for i in (1, 2, 0)):
            copy.wait_recv()
            yield ref


def reduce_steps(c, x, y, parts_a, parts_b, bufs, put_a, put_b, sent):
    ra, rb, qa, qb, ra2, rb2 = bufs
    dtype = qa.dtype
    sum_a = Sum(c, "row_1", x, parts_a, ra)
    sum_b = Sum(c, "row_0", y, parts_b, rb)
    yield
    va = sum_a.total().astype(dtype)
    for j in range(4):
        qa[j] = va[16 * j:16 * j + 16]
    sum_a2 = Sum(c, "row_0", y, qa, ra2)
    vb = sum_b.total().astype(dtype)
    for j in range(4):
        qb[j] = vb[16 * j:16 * j + 16]
    sum_b2 = Sum(c, "row_1", x, qb, rb2)
    yield
    put_a(sum_a2.total())
    put_b(sum_b2.total())
    for phase in (sum_a, sum_b, sum_a2, sum_b2):
        sent += phase.sent


def gather_steps(c, x, y, k, near_at, far_at, sent):
    near_a, near_b = near_at
    far_a, far_b = far_at
    shared = []

    def pair(ref):
        shared.append(c(ref, ref, {"row_2": 1 - k}))

    na = Spread(c, "row_0", y, near_a)
    nb = Spread(c, "row_1", x, near_b)
    yield
    for _ in na.each():
        pass
    fa = Spread(c, "row_1", x, far_a)
    for _ in nb.each():
        pass
    fb = Spread(c, "row_0", y, far_b)
    pair(far_a(x))
    pair(far_b(y))
    yield
    for refs in zip(fa.each(), fb.each()):
        for ref in refs:
            pair(ref)
    yield
    for copy in shared:
        copy.wait_recv()
    for phase in (na, nb, fa, fb):
        sent += phase.sent
    sent += shared


def kernel(threshold, g_hbm, w_hbm, d_hbm, x_out, dual_out,
           g_ref, w_v, d_v, wst, wt, wt2, g2, stat_s, stat_r, xd, wd, cp, pa, pb, fin, fil, gf, gh, gl, p0, p1, p2, uf, ub,
           ca, cb, cfin, bufs_g, bufs_c, in_sem, send, recv):
    z = lax.axis_index("grp")
    y = lax.axis_index("row_0")
    x = lax.axis_index("row_1")
    k = lax.axis_index("row_2")
    other = 1 - k
    c = Copies(send, recv)
    load_d = pltpu.make_async_copy(d_hbm, d_v, in_sem.at[0])
    load_w = pltpu.make_async_copy(w_hbm, w_v, in_sem.at[1])
    load_g = pltpu.make_async_copy(g_hbm, g_ref, in_sem.at[2])
    load_g.start()
    load_w.start()
    load_d.start()

    barrier = pltpu.get_barrier_semaphore()
    partner = {"row_2": other}
    plane = [{"row_0": turn(y, e, 4), "row_1": turn(x, d, 4), "row_2": turn(k, f, 2)}
             for e in range(4) for d in range(4) for f in range(2) if (e, d, f) != (0, 0, 0)]
    line = [{"grp": turn(z, d, 8)} for d in range(1, 8)]
    for peer in plane + line:
        pl.semaphore_signal(barrier, inc=1, device_id=peer, device_id_type=MESH)

    load_g.wait()
    g = g_ref[...]
    total = jnp.full((1, 128), jnp.sum(g * g), F32)
    stat_s[0] = total
    own = pl.ds(pl.multiple_of(128 * k, 128), 128)
    theirs = pl.ds(pl.multiple_of(128 * other, 128), 128)
    pl.semaphore_wait(barrier, len(plane) + len(line))
    stats = [c(stat_s.at[0], stat_r.at[i], peer) for i, peer in enumerate(plane)]
    pairs = [c(g_ref, g2, partner)]
    load_w.wait()
    w = w_v[...]
    wh = w.astype(BF16)
    wst[0:128] = wh
    wst[128:256] = (w - wh.astype(F32)).astype(BF16)
    wd[own] = wh
    pairs.append(c(wd.at[own], wd.at[own], partner))
    load_d.wait()

    def split(v):
        vh = v.astype(BF16)
        return vh, (v - vh.astype(F32)).astype(BF16)

    def weighted_chunk(j):
        cols = pl.ds(256 * j, 256)
        dh, dl = split(d_v[:, cols])
        both = jnp.dot(wst[...], dh, preferred_element_type=F32)
        acc = both[:128] + both[128:] + jnp.dot(wst[0:128], dl, preferred_element_type=F32)
        dh, dl = split(d_v[cols, :])
        dims = (((1,), (1,)), ((), ()))
        both = lax.dot_general(wst[...], dh, dims, preferred_element_type=F32)
        acc += both[:128] + both[128:]
        acc += lax.dot_general(wst[0:128], dl, dims, preferred_element_type=F32)
        wt[:, cols] = 0.5 * acc

    def half_weighted(m):
        for n in (2 * m, 2 * m + 1):
            weighted_chunk(n)
        cols = pl.ds(512 * m, 512)
        pairs.append(c(wt.at[:, cols], wt2.at[:, cols], partner))

    half_weighted(0)
    for i, copy in enumerate(stats):
        copy.wait_recv()
        total += stat_r[i]
    stat_s[1] = total
    lines = [c(stat_s.at[1], stat_r.at[31 + i], peer) for i, peer in enumerate(line)]
    half_weighted(1)
    for copy in pairs:
        copy.wait_recv()
    for i, copy in enumerate(lines):
        copy.wait_recv()
        total += stat_r[31 + i]

    clip = jnp.minimum(1.0, threshold * lax.rsqrt(total[0:1, 0:1]))
    for rows, ga, wa in ((own, g_ref, wt), (theirs, g2, wt2)):
        t = (clip * ga[...] + wa[...]).astype(BF16)
        xd[rows, 0:1024] = t
        xd[rows, 1024:1536] = t[:, 0:512]

    tn = (((0,), (0,)), ((), ()))
    for i in range(4):
        at = pl.multiple_of(128 * (2 * i + k), 128)
        part = lax.dot_general(
            xd[:, pl.ds(at, 128)], xd[:, pl.ds(at, WIN)], tn, preferred_element_type=F32)
        pa[i] = part[:64]
        pb[i] = part[64:]

    ended = []

    def put_gram(at_hi, at_lo):
        def put(v):
            hi = v.astype(BF16)
            at_hi[...] = hi
            at_lo[...] = (v - hi.astype(F32)).astype(BF16)
        return put

    near = lambda f: (lambda j: f.at[x, k, 0, j], lambda j: f.at[y, k, 1, j])
    far = lambda f: (lambda i: f.at[i, k, 0], lambda i: f.at[i, k, 1])
    gram_steps = reduce_steps(c, x, y, pa, pb, bufs_g,
                              put_gram(near(fin)[0](y), near(fil)[0](y)),
                              put_gram(near(fin)[1](x), near(fil)[1](x)), ended)
    next(gram_steps)
    for b in range(8):
        part = lax.dot_general(
            wd[:, 128 * b:128 * b + 128], xd[:, 0:1024], tn, preferred_element_type=F32)
        cp[b] = part.astype(BF16).reshape(2, 2, 2, 16, 1024)
    for e in range(4):
        for d in range(4):
            ca[d, 16 * e:16 * e + 16] = cp[2 * e + d // 2, d % 2, k, 0]
            cb[e, 16 * d:16 * d + 16] = cp[2 * e + d // 2, d % 2, k, 1]
    next(gram_steps)

    def put_at(ref):
        def put(v):
            ref[...] = v.astype(BF16)
        return put

    product_near = (lambda j: cfin.at[j, x, k, 0], lambda j: cfin.at[y, j, k, 1])
    product_far = (lambda i: cfin.at[:, i, k, 0], lambda i: cfin.at[i, :, k, 1])
    reduced = reduce_steps(c, x, y, ca, cb, bufs_c, put_at(product_near[0](y)),
                           put_at(product_near[1](x)), ended)
    gathered = gather_steps(c, x, y, k, product_near, product_far, ended)
    next(reduced)
    for _ in gram_steps:
        pass
    high = gather_steps(c, x, y, k, near(fin), far(fin), ended)
    low = gather_steps(c, x, y, k, near(fil), far(fil), ended)
    next(high)
    next(low)
    next(high)
    next(low)
    next(reduced)
    for _ in high:
        pass

    trace = jnp.zeros((1, 1), F32)
    eye = (lax.broadcasted_iota(jnp.int32, (128, 128), 0)
           == lax.broadcasted_iota(jnp.int32, (128, 128), 1))
    for b in range(8):
        i, core = b // 2, b % 2
        for j in range(5):
            m = (b + j) % 8
            block = fin[i, core, :, :, :, 128 * j:128 * j + 128].reshape(128, 128)
            rows, cols = pl.ds(128 * b, 128), pl.ds(128 * m, 128)
            gh[rows, cols] = block
            if j == 0:
                trace += jnp.sum(jnp.where(eye, block.astype(F32), 0.0), keepdims=True)
            if 0 < j < 4:
                gh[cols, rows] = block.T
    scale = 1.0 / (trace + epsilon)
    root = jnp.sqrt(scale)

    def dot(u, v):
        return jnp.dot(u, v, preferred_element_type=F32)

    TILE = 256
    tiles = [pl.ds(TILE * n, TILE) for n in range(1024 // TILE)]
    done = [0]

    def advance():
        done[0] += 1
        for steps in STEPS.get(done[0], ()):
            next((low, reduced, gathered)[steps], None)

    def square(p, n, s):
        g = gh[:, n].astype(F32) if p is p0 else gf[:, n]
        p[:, n] = ((coef_b * s) * g + (coef_c * s * s) * dot(gh[...], gh[:, n])).astype(BF16)
        advance()

    def left(p, n):
        g = gh[:, n].astype(F32) if p is p0 else gf[:, n]
        u = coef_a * g + dot(p[...], gh[:, n])
        uf[:, n] = u
        ub[:, n] = u.astype(BF16)
        advance()

    def right(p, n, s):
        v = coef_a * uf[:, n] + dot(ub[...], p[:, n])
        if p is p0:
            v = s * (v + (coef_a * coef_a) * gl[:, n].astype(F32))
        gf[:, n] = v
        gh[:, n] = v.astype(BF16)
        advance()

    for n in tiles:
        square(p0, n, scale)
    for n in tiles:
        left(p0, n)
    for _ in low:
        pass
    for b in range(8):
        i, core = b // 2, b % 2
        for j in range(5):
            m = (b + j) % 8
            block = fil[i, core, :, :, :, 128 * j:128 * j + 128].reshape(128, 128)
            rows, cols = pl.ds(128 * b, 128), pl.ds(128 * m, 128)
            gl[rows, cols] = block
            if 0 < j < 4:
                gl[cols, rows] = block.T
    for n in tiles:
        right(p0, n, scale)
    for n in tiles:
        square(p1, n, 1.0)
    for n in tiles:
        left(p1, n)
    for n in tiles:
        right(p1, n, 1.0)
    for n in tiles:
        square(p2, n, 1.0)

    mine = cfin[y, x, k].reshape(32, 1024)
    share = 8 * y + 2 * x + k
    unit = (lax.broadcasted_iota(jnp.int32, (32, 1024), 0) + 32 * share
            == lax.broadcasted_iota(jnp.int32, (32, 1024), 1))
    stack = jnp.concatenate([xd[own, 0:1024], mine, unit.astype(F32).astype(BF16)], axis=0)
    v = coef_a * stack.astype(F32) + dot(stack, p0[...])
    v = coef_a * v + dot(v.astype(BF16), p1[...])
    v = coef_a * v + dot(v.astype(BF16), p2[...])

    def by_gram(v):
        v = dot((coef_a * v + dot(v.astype(BF16), p2[...])).astype(BF16), gh[...])
        return coef_a * v + dot(v.astype(BF16), p2[...])

    once = by_gram(v)
    v = coef_a * v + coef_b * once + coef_c * by_gram(once)
    for _ in gathered:
        pass
    x_out[...] = (root * v[0:128]).astype(BF16)
    cross = v[128:160] + lax.dot_general(
        v[160:192].astype(BF16), cfin[...].reshape(1024, 1024), (((1,), (1,)), ((), ())),
        preferred_element_type=F32)
    dual_out[...] = d_v[pl.ds(pl.multiple_of(32 * share, 32), 32), :] - (16.0 * root) * cross

    for copy in stats + lines + pairs + ended:
        copy.wait_send()


def step_of(gradient, weight, dual, threshold):
    vmem = lambda *s: pltpu.VMEM(s, F32)
    half = lambda *s: pltpu.VMEM(s, BF16)

    def bufs(kind, width):
        first, second = kind(3, 64, width), kind(3, 16, width)
        return [first, first, kind(4, 16, width), kind(4, 16, width), second, second]

    n_copies = 38 + 4 + 12 * 2 + 20 * 3
    return pl.pallas_call(
        lambda *refs: kernel(threshold, *refs),
        out_shape=(jax.ShapeDtypeStruct((128, 1024), BF16),
                   jax.ShapeDtypeStruct((32, 1024), F32)),
        in_specs=[pl.BlockSpec(memory_space=pltpu.HBM)] * 3,
        out_specs=[pl.BlockSpec(memory_space=pltpu.VMEM)] * 2,
        scratch_shapes=[
            vmem(128, 1024), vmem(128, 1024), vmem(1024, 1024), half(256, 1024), vmem(128, 1024),
            vmem(128, 1024), vmem(128, 1024), vmem(2, 1, 128), vmem(38, 1, 128), half(256, 1536), half(256, 1024),
            half(8, 2, 2, 2, 16, 1024),
            vmem(4, 64, WIN), vmem(4, 64, WIN), half(4, 2, 2, 4, 16, WIN), half(4, 2, 2, 4, 16, WIN),
            vmem(1024, 1024), half(1024, 1024), half(1024, 1024), half(1024, 1024), half(1024, 1024),
            half(1024, 1024), vmem(1024, 1024), half(1024, 1024),
            half(4, 64, 1024), half(4, 64, 1024), half(4, 4, 2, 2, 16, 1024),
            bufs(vmem, WIN), bufs(half, 1024),
            pltpu.SemaphoreType.DMA((3,)), pltpu.SemaphoreType.DMA((n_copies,)),
            pltpu.SemaphoreType.DMA((n_copies,)),
        ],
        compiler_params=pltpu.CompilerParams(
            collective_id=0, has_side_effects=True, vmem_limit_bytes=59000 * 1024),
        name="step",
    )(gradient, weight, dual)


def local(gradient, weight, dual):
    local_rows, col_count = gradient.shape[1:]
    threshold = 0.5 * math.sqrt(
        local_rows * lax.axis_size(ROW) * col_count * lax.axis_size("grp"))
    iterate, dual_next = step_of(gradient[0], weight[0], dual[0], threshold)
    update = math.sqrt(col_count) * iterate.astype(F32)
    return (update[None], dual_next[None])


def solution(mesh):
    torus = Mesh(
        mesh.devices.reshape(mesh.shape["grp"], 4, 4, 2), ("grp", "row_0", "row_1", "row_2")
    )
    in_specs = (P("grp", ROW, None), P("grp", ROW, None), P("grp", None, None))
    out_specs = (P("grp", ROW, None), P("grp", ROW, None))
    return jax.shard_map(local, mesh=torus, in_specs=in_specs, out_specs=out_specs, check_vma=False)
```

```python
import math

import jax
import jax.numpy as jnp
from jax import lax
from jax.experimental import pallas as pl
from jax.experimental.pallas import tpu as pltpu
from jax.sharding import Mesh
from jax.sharding import PartitionSpec as P

ROW = ("row_0", "row_1", "row_2")
MESH = pl.DeviceIdType.MESH
coef_a = 3.4445
coef_b = -4.775
coef_c = 2.0315
epsilon = 1e-06
WIN = 640
STEPS = {3: (1, 2), 4: (0,), 13: (2,)}
F32 = jnp.float32
BF16 = jnp.bfloat16


class Copies:
    def __init__(self, send, recv):
        self.send, self.recv, self.n = send, recv, 0

    def __call__(self, src, dst, where):
        i = self.n
        self.n += 1
        copy = pltpu.make_async_remote_copy(
            src_ref=src, dst_ref=dst, send_sem=self.send.at[i], recv_sem=self.recv.at[i],
            device_id=where, device_id_type=MESH,
        )
        copy.start()
        return copy


def turn(p, d, n):
    return lax.rem(p + d, n)


class Sum:
    def __init__(self, copies, axis, p, part, arrived, dist=(2, 1, 3)):
        self.copies, self.axis = copies, axis
        self.p, self.part, self.arrived = p, part, arrived
        self.sent = []
        self.send(dist)

    def send(self, dist):
        for d in dist:
            to = turn(self.p, d, 4)
            self.sent.append(
                self.copies(self.part.at[to], self.arrived.at[d - 1], {self.axis: to}))

    def total(self):
        for copy in self.sent:
            copy.wait_recv()
        out = self.part[self.p].astype(F32)
        for d in range(3):
            out += self.arrived[d].astype(F32)
        return out


class Spread:
    def __init__(self, copies, axis, p, at):
        self.sent = [copies(at(p), at(p), {axis: turn(p, d, 4)}) for d in (2, 1, 3)]
        self.came = [at(turn(p, 4 - d, 4)) for d in (2, 1, 3)]

    def each(self):
        for copy, ref in ((self.sent[i], self.came[i]) for i in (1, 2, 0)):
            copy.wait_recv()
            yield ref


def reduce_steps(c, x, y, parts_a, parts_b, bufs, put_a, put_b, sent, split=False):
    ra, rb, qa, qb, ra2, rb2 = bufs
    dtype = qa.dtype
    first = (2,) if split else (2, 1, 3)
    sum_a = Sum(c, "row_1", x, parts_a, ra, first)
    sum_b = Sum(c, "row_0", y, parts_b, rb, first)
    yield
    if split:
        sum_a.send((1, 3))
        sum_b.send((1, 3))
        yield
    va = sum_a.total().astype(dtype)
    for j in range(4):
        qa[j] = va[16 * j:16 * j + 16]
    sum_a2 = Sum(c, "row_0", y, qa, ra2)
    vb = sum_b.total().astype(dtype)
    for j in range(4):
        qb[j] = vb[16 * j:16 * j + 16]
    sum_b2 = Sum(c, "row_1", x, qb, rb2)
    yield
    put_a(sum_a2.total())
    put_b(sum_b2.total())
    for phase in (sum_a, sum_b, sum_a2, sum_b2):
        sent += phase.sent


def gather_steps(c, x, y, k, near_at, far_at, sent):
    near_a, near_b = near_at
    far_a, far_b = far_at
    shared = []

    def pair(ref):
        shared.append(c(ref, ref, {"row_2": 1 - k}))

    na = Spread(c, "row_0", y, near_a)
    nb = Spread(c, "row_1", x, near_b)
    yield
    for _ in na.each():
        pass
    fa = Spread(c, "row_1", x, far_a)
    for _ in nb.each():
        pass
    fb = Spread(c, "row_0", y, far_b)
    pair(far_a(x))
    pair(far_b(y))
    yield
    for refs in zip(fa.each(), fb.each()):
        for ref in refs:
            pair(ref)
    yield
    for copy in shared:
        copy.wait_recv()
    for phase in (na, nb, fa, fb):
        sent += phase.sent
    sent += shared


def kernel(threshold, g_hbm, w_hbm, d_hbm, x_out, dual_out,
           g_ref, w_v, d_v, wst, wt, wt2, g2, stat_s, stat_r, xd, wd, cp, pa, pb, fin, fil, gf, gh, gl, p0, p1, p2, uf, ub,
           ca, cb, cfin, bufs_g, bufs_c, in_sem, send, recv):
    z = lax.axis_index("grp")
    y = lax.axis_index("row_0")
    x = lax.axis_index("row_1")
    k = lax.axis_index("row_2")
    other = 1 - k
    c = Copies(send, recv)
    load_d = pltpu.make_async_copy(d_hbm, d_v, in_sem.at[0])
    load_w = pltpu.make_async_copy(w_hbm, w_v, in_sem.at[1])
    load_g = pltpu.make_async_copy(g_hbm, g_ref, in_sem.at[2])
    load_g.start()
    load_w.start()
    load_d.start()

    barrier = pltpu.get_barrier_semaphore()
    partner = {"row_2": other}
    plane = [{"row_0": turn(y, e, 4), "row_1": turn(x, d, 4), "row_2": turn(k, f, 2)}
             for e in range(4) for d in range(4) for f in range(2) if (e, d, f) != (0, 0, 0)]
    line = [{"grp": turn(z, d, 8)} for d in range(1, 8)]
    for peer in plane + line:
        pl.semaphore_signal(barrier, inc=1, device_id=peer, device_id_type=MESH)

    load_g.wait()
    g = g_ref[...]
    total = jnp.full((1, 128), jnp.sum(g * g), F32)
    stat_s[0] = total
    own = pl.ds(pl.multiple_of(128 * k, 128), 128)
    theirs = pl.ds(pl.multiple_of(128 * other, 128), 128)
    pl.semaphore_wait(barrier, len(plane) + len(line))
    stats = [c(stat_s.at[0], stat_r.at[i], peer) for i, peer in enumerate(plane)]
    pairs = [c(g_ref, g2, partner)]
    load_w.wait()
    w = w_v[...]
    wh = w.astype(BF16)
    wst[0:128] = wh
    wst[128:256] = (w - wh.astype(F32)).astype(BF16)
    wd[own] = wh
    pairs.append(c(wd.at[own], wd.at[own], partner))
    load_d.wait()

    def split(v):
        vh = v.astype(BF16)
        return vh, (v - vh.astype(F32)).astype(BF16)

    def weighted_chunk(j):
        cols = pl.ds(256 * j, 256)
        dh, dl = split(d_v[:, cols])
        both = jnp.dot(wst[...], dh, preferred_element_type=F32)
        acc = both[:128] + both[128:] + jnp.dot(wst[0:128], dl, preferred_element_type=F32)
        dh, dl = split(d_v[cols, :])
        dims = (((1,), (1,)), ((), ()))
        both = lax.dot_general(wst[...], dh, dims, preferred_element_type=F32)
        acc += both[:128] + both[128:]
        acc += lax.dot_general(wst[0:128], dl, dims, preferred_element_type=F32)
        wt[:, cols] = 0.5 * acc

    def half_weighted(m):
        for n in (2 * m, 2 * m + 1):
            weighted_chunk(n)
        cols = pl.ds(512 * m, 512)
        pairs.append(c(wt.at[:, cols], wt2.at[:, cols], partner))

    half_weighted(0)
    for i, copy in enumerate(stats):
        copy.wait_recv()
        total += stat_r[i]
    stat_s[1] = total
    lines = [c(stat_s.at[1], stat_r.at[31 + i], peer) for i, peer in enumerate(line)]
    half_weighted(1)
    for copy in pairs:
        copy.wait_recv()
    for i, copy in enumerate(lines):
        copy.wait_recv()
        total += stat_r[31 + i]

    clip = jnp.minimum(1.0, threshold * lax.rsqrt(total[0:1, 0:1]))
    for rows, ga, wa in ((own, g_ref, wt), (theirs, g2, wt2)):
        t = (clip * ga[...] + wa[...]).astype(BF16)
        xd[rows, 0:1024] = t
        xd[rows, 1024:1536] = t[:, 0:512]

    tn = (((0,), (0,)), ((), ()))
    for i in range(4):
        at = pl.multiple_of(128 * (2 * i + k), 128)
        part = lax.dot_general(
            xd[:, pl.ds(at, 128)], xd[:, pl.ds(at, WIN)], tn, preferred_element_type=F32)
        pa[i] = part[:64]
        pb[i] = part[64:]

    ended = []

    def put_gram(at_hi, at_lo):
        def put(v):
            hi = v.astype(BF16)
            at_hi[...] = hi
            at_lo[...] = (v - hi.astype(F32)).astype(BF16)
        return put

    near = lambda f: (lambda j: f.at[x, k, 0, j], lambda j: f.at[y, k, 1, j])
    far = lambda f: (lambda i: f.at[i, k, 0], lambda i: f.at[i, k, 1])
    gram_steps = reduce_steps(c, x, y, pa, pb, bufs_g,
                              put_gram(near(fin)[0](y), near(fil)[0](y)),
                              put_gram(near(fin)[1](x), near(fil)[1](x)), ended)
    next(gram_steps)
    for b in range(8):
        part = lax.dot_general(
            wd[:, 128 * b:128 * b + 128], xd[:, 0:1024], tn, preferred_element_type=F32)
        cp[b] = part.astype(BF16).reshape(2, 2, 2, 16, 1024)
    for e in range(4):
        for d in range(4):
            ca[d, 16 * e:16 * e + 16] = cp[2 * e + d // 2, d % 2, k, 0]
            cb[e, 16 * d:16 * d + 16] = cp[2 * e + d // 2, d % 2, k, 1]
    next(gram_steps)

    def put_at(ref):
        def put(v):
            ref[...] = v.astype(BF16)
        return put

    product_near = (lambda j: cfin.at[j, x, k, 0], lambda j: cfin.at[y, j, k, 1])
    product_far = (lambda i: cfin.at[:, i, k, 0], lambda i: cfin.at[i, :, k, 1])
    reduced = reduce_steps(c, x, y, ca, cb, bufs_c, put_at(product_near[0](y)),
                           put_at(product_near[1](x)), ended, True)
    gathered = gather_steps(c, x, y, k, product_near, product_far, ended)
    next(reduced)
    for _ in gram_steps:
        pass
    high = gather_steps(c, x, y, k, near(fin), far(fin), ended)
    low = gather_steps(c, x, y, k, near(fil), far(fil), ended)
    next(high)
    next(low)
    next(reduced)
    next(high)
    next(low)
    next(reduced)
    for _ in high:
        pass

    trace = jnp.zeros((1, 1), F32)
    eye = (lax.broadcasted_iota(jnp.int32, (128, 128), 0)
           == lax.broadcasted_iota(jnp.int32, (128, 128), 1))
    for b in range(8):
        i, core = b // 2, b % 2
        for j in range(5):
            m = (b + j) % 8
            block = fin[i, core, :, :, :, 128 * j:128 * j + 128].reshape(128, 128)
            rows, cols = pl.ds(128 * b, 128), pl.ds(128 * m, 128)
            gh[rows, cols] = block
            if j == 0:
                trace += jnp.sum(jnp.where(eye, block.astype(F32), 0.0), keepdims=True)
            if 0 < j < 4:
                gh[cols, rows] = block.T
    scale = 1.0 / (trace + epsilon)
    root = jnp.sqrt(scale)

    def dot(u, v):
        return jnp.dot(u, v, preferred_element_type=F32)

    TILE = 256
    tiles = [pl.ds(TILE * n, TILE) for n in range(1024 // TILE)]
    done = [0]

    def advance():
        done[0] += 1
        for steps in STEPS.get(done[0], ()):
            next((low, reduced, gathered)[steps], None)

    def square(p, n, s):
        g = gh[:, n].astype(F32) if p is p0 else gf[:, n]
        p[:, n] = ((coef_b * s) * g + (coef_c * s * s) * dot(gh[...], gh[:, n])).astype(BF16)
        advance()

    def left(p, n):
        g = gh[:, n].astype(F32) if p is p0 else gf[:, n]
        u = coef_a * g + dot(p[...], gh[:, n])
        uf[:, n] = u
        ub[:, n] = u.astype(BF16)
        advance()

    def right(p, n, s):
        v = coef_a * uf[:, n] + dot(ub[...], p[:, n])
        if p is p0:
            v = s * (v + (coef_a * coef_a) * gl[:, n].astype(F32))
        gf[:, n] = v
        gh[:, n] = v.astype(BF16)
        advance()

    for n in tiles:
        square(p0, n, scale)
    for n in tiles:
        left(p0, n)
    for _ in low:
        pass
    for b in range(8):
        i, core = b // 2, b % 2
        for j in range(5):
            m = (b + j) % 8
            block = fil[i, core, :, :, :, 128 * j:128 * j + 128].reshape(128, 128)
            rows, cols = pl.ds(128 * b, 128), pl.ds(128 * m, 128)
            gl[rows, cols] = block
            if 0 < j < 4:
                gl[cols, rows] = block.T
    for n in tiles:
        right(p0, n, scale)
    for n in tiles:
        square(p1, n, 1.0)
    for n in tiles:
        left(p1, n)
    for n in tiles:
        right(p1, n, 1.0)
    for n in tiles:
        square(p2, n, 1.0)

    mine = cfin[y, x, k].reshape(32, 1024)
    share = 8 * y + 2 * x + k
    unit = (lax.broadcasted_iota(jnp.int32, (32, 1024), 0) + 32 * share
            == lax.broadcasted_iota(jnp.int32, (32, 1024), 1))
    stack = jnp.concatenate([xd[own, 0:1024], mine, unit.astype(F32).astype(BF16)], axis=0)
    v = coef_a * stack.astype(F32) + dot(stack, p0[...])
    v = coef_a * v + dot(v.astype(BF16), p1[...])
    v = coef_a * v + dot(v.astype(BF16), p2[...])

    def by_gram(v):
        v = dot((coef_a * v + dot(v.astype(BF16), p2[...])).astype(BF16), gh[...])
        return coef_a * v + dot(v.astype(BF16), p2[...])

    next(gathered)
    once = by_gram(v)
    v = coef_a * v + coef_b * once + coef_c * by_gram(once)
    for _ in gathered:
        pass
    x_out[...] = (root * v[0:128]).astype(BF16)
    cross = v[128:160] + lax.dot_general(
        v[160:192].astype(BF16), cfin[...].reshape(1024, 1024), (((1,), (1,)), ((), ())),
        preferred_element_type=F32)
    dual_out[...] = d_v[pl.ds(pl.multiple_of(32 * share, 32), 32), :] - (16.0 * root) * cross

    for copy in stats + lines + pairs + ended:
        copy.wait_send()


def step_of(gradient, weight, dual, threshold):
    vmem = lambda *s: pltpu.VMEM(s, F32)
    half = lambda *s: pltpu.VMEM(s, BF16)

    def bufs(kind, width):
        first, second = kind(3, 64, width), kind(3, 16, width)
        return [first, first, kind(4, 16, width), kind(4, 16, width), second, second]

    n_copies = 38 + 4 + 12 * 2 + 20 * 3
    return pl.pallas_call(
        lambda *refs: kernel(threshold, *refs),
        out_shape=(jax.ShapeDtypeStruct((128, 1024), BF16),
                   jax.ShapeDtypeStruct((32, 1024), F32)),
        in_specs=[pl.BlockSpec(memory_space=pltpu.HBM)] * 3,
        out_specs=[pl.BlockSpec(memory_space=pltpu.VMEM)] * 2,
        scratch_shapes=[
            vmem(128, 1024), vmem(128, 1024), vmem(1024, 1024), half(256, 1024), vmem(128, 1024),
            vmem(128, 1024), vmem(128, 1024), vmem(2, 1, 128), vmem(38, 1, 128), half(256, 1536), half(256, 1024),
            half(8, 2, 2, 2, 16, 1024),
            vmem(4, 64, WIN), vmem(4, 64, WIN), half(4, 2, 2, 4, 16, WIN), half(4, 2, 2, 4, 16, WIN),
            vmem(1024, 1024), half(1024, 1024), half(1024, 1024), half(1024, 1024), half(1024, 1024),
            half(1024, 1024), vmem(1024, 1024), half(1024, 1024),
            half(4, 64, 1024), half(4, 64, 1024), half(4, 4, 2, 2, 16, 1024),
            bufs(vmem, WIN), bufs(half, 1024),
            pltpu.SemaphoreType.DMA((3,)), pltpu.SemaphoreType.DMA((n_copies,)),
            pltpu.SemaphoreType.DMA((n_copies,)),
        ],
        compiler_params=pltpu.CompilerParams(
            collective_id=0, has_side_effects=True, vmem_limit_bytes=59000 * 1024),
        name="step",
    )(gradient, weight, dual)


def local(gradient, weight, dual):
    local_rows, col_count = gradient.shape[1:]
    threshold = 0.5 * math.sqrt(
        local_rows * lax.axis_size(ROW) * col_count * lax.axis_size("grp"))
    iterate, dual_next = step_of(gradient[0], weight[0], dual[0], threshold)
    update = math.sqrt(col_count) * iterate.astype(F32)
    return (update[None], dual_next[None])


def solution(mesh):
    torus = Mesh(
        mesh.devices.reshape(mesh.shape["grp"], 4, 4, 2), ("grp", "row_0", "row_1", "row_2")
    )
    in_specs = (P("grp", ROW, None), P("grp", ROW, None), P("grp", None, None))
    out_specs = (P("grp", ROW, None), P("grp", ROW, None))
    return jax.shard_map(local, mesh=torus, in_specs=in_specs, out_specs=out_specs, check_vma=False)
```

```python
import functools
import math

import jax
import jax.numpy as jnp
from jax import lax
from jax.experimental import pallas as pl
from jax.experimental.pallas import tpu as pltpu
from jax.sharding import Mesh
from jax.sharding import PartitionSpec as P

ROW = ("row_0", "row_1", "row_2")
MESH = pl.DeviceIdType.MESH
coef_a = 3.4445
coef_b = -4.775
coef_c = 2.0315
epsilon = 1e-06
WIN = 640
STEPS = {4: (0,), 8: (1,), 16: (1, 2), 23: (2,)}
F32 = jnp.float32
BF16 = jnp.bfloat16


class Copies:
    def __init__(self, send, recv):
        self.send, self.recv, self.n = send, recv, 0

    def __call__(self, src, dst, where):
        i = self.n
        self.n += 1
        copy = pltpu.make_async_remote_copy(
            src_ref=src, dst_ref=dst, send_sem=self.send.at[i], recv_sem=self.recv.at[i],
            device_id=where, device_id_type=MESH,
        )
        copy.start()
        return copy


def turn(p, d, n):
    return lax.rem(p + d, n)


class Sum:
    def __init__(self, copies, axis, p, part, arrived, dist=(2, 1, 3)):
        self.copies, self.axis = copies, axis
        self.p, self.part, self.arrived = p, part, arrived
        self.sent = []
        self.send(dist)

    def send(self, dist):
        for d in dist:
            to = turn(self.p, d, 4)
            self.sent.append(
                self.copies(self.part.at[to], self.arrived.at[d - 1], {self.axis: to}))

    def total(self):
        for copy in self.sent:
            copy.wait_recv()
        out = self.part[self.p].astype(F32)
        for d in range(3):
            out += self.arrived[d].astype(F32)
        return out


class Spread:
    def __init__(self, copies, axis, p, at):
        self.sent = [copies(at(p), at(p), {axis: turn(p, d, 4)}) for d in (2, 1, 3)]
        self.came = [at(turn(p, 4 - d, 4)) for d in (2, 1, 3)]

    def each(self):
        for copy, ref in ((self.sent[i], self.came[i]) for i in (1, 2, 0)):
            copy.wait_recv()
            yield ref


def reduce_steps(c, x, y, parts_a, parts_b, bufs, put_a, put_b, sent, split=False):
    ra, rb, qa, qb, ra2, rb2 = bufs
    dtype = qa.dtype
    first = (2,) if split else (2, 1, 3)
    sum_a = Sum(c, "row_1", x, parts_a, ra, first)
    sum_b = Sum(c, "row_0", y, parts_b, rb, first)
    yield
    if split:
        sum_a.send((1, 3))
        sum_b.send((1, 3))
        yield
    va = sum_a.total().astype(dtype)
    for j in range(4):
        qa[j] = va[16 * j:16 * j + 16]
    sum_a2 = Sum(c, "row_0", y, qa, ra2)
    vb = sum_b.total().astype(dtype)
    for j in range(4):
        qb[j] = vb[16 * j:16 * j + 16]
    sum_b2 = Sum(c, "row_1", x, qb, rb2)
    yield
    put_a(sum_a2.total())
    put_b(sum_b2.total())
    for phase in (sum_a, sum_b, sum_a2, sum_b2):
        sent += phase.sent


def gather_steps(c, x, y, k, near_at, far_at, sent):
    near_a, near_b = near_at
    far_a, far_b = far_at
    shared = []

    def pair(ref):
        shared.append(c(ref, ref, {"row_2": 1 - k}))

    na = Spread(c, "row_0", y, near_a)
    nb = Spread(c, "row_1", x, near_b)
    yield
    for _ in na.each():
        pass
    fa = Spread(c, "row_1", x, far_a)
    for _ in nb.each():
        pass
    fb = Spread(c, "row_0", y, far_b)
    pair(far_a(x))
    pair(far_b(y))
    yield
    for refs in zip(fa.each(), fb.each()):
        for ref in refs:
            pair(ref)
    yield
    for copy in shared:
        copy.wait_recv()
    for phase in (na, nb, fa, fb):
        sent += phase.sent
    sent += shared


def kernel(threshold, g_hbm, w_hbm, d_hbm, x_out, dual_out,
           g_ref, w_v, d_v, wst, wt, wt2, g2, stat_s, stat_r, xd, wd, cp, pa, pb, fin, fil, gf, gh, gl, p0, p1, p2, uf, ub,
           ca, cb, cfin, bufs_g, bufs_c, in_sem, send, recv):
    z = lax.axis_index("grp")
    y = lax.axis_index("row_0")
    x = lax.axis_index("row_1")
    k = lax.axis_index("row_2")
    other = 1 - k
    c = Copies(send, recv)
    load_d = pltpu.make_async_copy(d_hbm, d_v, in_sem.at[0])
    load_w = pltpu.make_async_copy(w_hbm, w_v, in_sem.at[1])
    load_g = pltpu.make_async_copy(g_hbm, g_ref, in_sem.at[2])
    load_g.start()
    load_w.start()
    load_d.start()

    barrier = pltpu.get_barrier_semaphore()
    partner = {"row_2": other}
    plane = [{"row_0": turn(y, e, 4), "row_1": turn(x, d, 4), "row_2": turn(k, f, 2)}
             for e in range(4) for d in range(4) for f in range(2) if (e, d, f) != (0, 0, 0)]
    line = [{"grp": turn(z, d, 8)} for d in range(1, 8)]
    for peer in plane + line:
        pl.semaphore_signal(barrier, inc=1, device_id=peer, device_id_type=MESH)

    load_g.wait()
    g = g_ref[...]
    total = jnp.full((1, 128), jnp.sum(g * g), F32)
    stat_s[0] = total
    own = pl.ds(pl.multiple_of(128 * k, 128), 128)
    theirs = pl.ds(pl.multiple_of(128 * other, 128), 128)
    pl.semaphore_wait(barrier, len(plane) + len(line))
    stats = [c(stat_s.at[0], stat_r.at[i], peer) for i, peer in enumerate(plane)]
    pairs = [c(g_ref, g2, partner)]
    load_w.wait()
    w = w_v[...]
    wh = w.astype(BF16)
    wst[0:128] = wh
    wst[128:256] = (w - wh.astype(F32)).astype(BF16)
    wd[own] = wh
    pairs.append(c(wd.at[own], wd.at[own], partner))
    load_d.wait()

    def split(v):
        vh = v.astype(BF16)
        return vh, (v - vh.astype(F32)).astype(BF16)

    def weighted_chunk(j):
        cols = pl.ds(256 * j, 256)
        dh, dl = split(d_v[:, cols])
        both = jnp.dot(wst[...], dh, preferred_element_type=F32)
        acc = both[:128] + both[128:] + jnp.dot(wst[0:128], dl, preferred_element_type=F32)
        dh, dl = split(d_v[cols, :])
        dims = (((1,), (1,)), ((), ()))
        both = lax.dot_general(wst[...], dh, dims, preferred_element_type=F32)
        acc += both[:128] + both[128:]
        acc += lax.dot_general(wst[0:128], dl, dims, preferred_element_type=F32)
        wt[:, cols] = 0.5 * acc

    def half_weighted(m):
        for n in (2 * m, 2 * m + 1):
            weighted_chunk(n)
        cols = pl.ds(512 * m, 512)
        pairs.append(c(wt.at[:, cols], wt2.at[:, cols], partner))

    half_weighted(0)
    for i, copy in enumerate(stats):
        copy.wait_recv()
        total += stat_r[i]
    stat_s[1] = total
    lines = [c(stat_s.at[1], stat_r.at[31 + i], peer) for i, peer in enumerate(line)]
    half_weighted(1)
    for copy in pairs:
        copy.wait_recv()
    for i, copy in enumerate(lines):
        copy.wait_recv()
        total += stat_r[31 + i]

    clip = jnp.minimum(1.0, threshold * lax.rsqrt(total[0:1, 0:1]))
    for rows, ga, wa in ((own, g_ref, wt), (theirs, g2, wt2)):
        t = (clip * ga[...] + wa[...]).astype(BF16)
        xd[rows, 0:1024] = t
        xd[rows, 1024:1536] = t[:, 0:512]

    tn = (((0,), (0,)), ((), ()))
    for i in range(4):
        at = pl.multiple_of(128 * (2 * i + k), 128)
        part = lax.dot_general(
            xd[:, pl.ds(at, 128)], xd[:, pl.ds(at, WIN)], tn, preferred_element_type=F32)
        pa[i] = part[:64]
        pb[i] = part[64:]

    ended = []

    def put_gram(at_hi, at_lo):
        def put(v):
            hi = v.astype(BF16)
            at_hi[...] = hi
            at_lo[...] = (v - hi.astype(F32)).astype(BF16)
        return put

    near = lambda f: (lambda j: f.at[x, k, 0, j], lambda j: f.at[y, k, 1, j])
    far = lambda f: (lambda i: f.at[i, k, 0], lambda i: f.at[i, k, 1])
    gram_steps = reduce_steps(c, x, y, pa, pb, bufs_g,
                              put_gram(near(fin)[0](y), near(fil)[0](y)),
                              put_gram(near(fin)[1](x), near(fil)[1](x)), ended)
    next(gram_steps)
    for b in range(8):
        part = lax.dot_general(
            wd[:, 128 * b:128 * b + 128], xd[:, 0:1024], tn, preferred_element_type=F32)
        cp[b] = part.astype(BF16).reshape(2, 2, 2, 16, 1024)
    for e in range(4):
        for d in range(4):
            ca[d, 16 * e:16 * e + 16] = cp[2 * e + d // 2, d % 2, k, 0]
            cb[e, 16 * d:16 * d + 16] = cp[2 * e + d // 2, d % 2, k, 1]
    next(gram_steps)

    def put_at(ref):
        def put(v):
            ref[...] = v.astype(BF16)
        return put

    product_near = (lambda j: cfin.at[j, x, k, 0], lambda j: cfin.at[y, j, k, 1])
    product_far = (lambda i: cfin.at[:, i, k, 0], lambda i: cfin.at[i, :, k, 1])
    reduced = reduce_steps(c, x, y, ca, cb, bufs_c, put_at(product_near[0](y)),
                           put_at(product_near[1](x)), ended, True)
    gathered = gather_steps(c, x, y, k, product_near, product_far, ended)
    for _ in gram_steps:
        pass
    high = gather_steps(c, x, y, k, near(fin), far(fin), ended)
    low = gather_steps(c, x, y, k, near(fil), far(fil), ended)
    next(high)
    next(low)
    next(high)
    next(low)
    next(reduced)
    next(reduced)
    for _ in high:
        pass

    trace = jnp.zeros((1, 1), F32)
    eye = (lax.broadcasted_iota(jnp.int32, (128, 128), 0)
           == lax.broadcasted_iota(jnp.int32, (128, 128), 1))
    for b in range(8):
        i, core = b // 2, b % 2
        for j in range(5):
            m = (b + j) % 8
            block = fin[i, core, :, :, :, 128 * j:128 * j + 128].reshape(128, 128)
            rows, cols = pl.ds(128 * b, 128), pl.ds(128 * m, 128)
            gh[rows, cols] = block
            if j == 0:
                trace += jnp.sum(jnp.where(eye, block.astype(F32), 0.0), keepdims=True)
            if 0 < j < 4:
                gh[cols, rows] = block.T
    scale = 1.0 / (trace + epsilon)
    root = jnp.sqrt(scale)

    def dot(u, v):
        return jnp.dot(u, v, preferred_element_type=F32)

    TILE = 256
    tiles = [pl.ds(TILE * n, TILE) for n in range(1024 // TILE)]
    done = [0]

    def advance():
        done[0] += 1
        for steps in STEPS.get(done[0], ()):
            next((low, reduced, gathered)[steps], None)

    def square(p, n, s):
        g = gh[:, n].astype(F32) if p is p0 else gf[:, n]
        p[:, n] = ((coef_b * s) * g + (coef_c * s * s) * dot(gh[...], gh[:, n])).astype(BF16)
        advance()

    def left(p, n):
        g = gh[:, n].astype(F32) if p is p0 else gf[:, n]
        u = coef_a * g + dot(p[...], gh[:, n])
        uf[:, n] = u
        ub[:, n] = u.astype(BF16)
        advance()

    def right(p, n, s):
        v = coef_a * uf[:, n] + dot(ub[...], p[:, n])
        if p is p0:
            v = s * (v + (coef_a * coef_a) * gl[:, n].astype(F32))
        gf[:, n] = v
        gh[:, n] = v.astype(BF16)
        advance()

    for n in tiles:
        square(p0, n, scale)
    for n in tiles:
        left(p0, n)
    for _ in low:
        pass
    for b in range(8):
        i, core = b // 2, b % 2
        for j in range(5):
            m = (b + j) % 8
            block = fil[i, core, :, :, :, 128 * j:128 * j + 128].reshape(128, 128)
            rows, cols = pl.ds(128 * b, 128), pl.ds(128 * m, 128)
            gl[rows, cols] = block
            if 0 < j < 4:
                gl[cols, rows] = block.T
    for n in tiles:
        right(p0, n, scale)
    for n in tiles:
        square(p1, n, 1.0)
    for n in tiles:
        left(p1, n)
    for n in tiles:
        right(p1, n, 1.0)
    for n in tiles:
        square(p2, n, 1.0)

    mine = cfin[y, x, k].reshape(32, 1024)
    share = 8 * y + 2 * x + k
    unit = (lax.broadcasted_iota(jnp.int32, (32, 1024), 0) + 32 * share
            == lax.broadcasted_iota(jnp.int32, (32, 1024), 1))
    stack = jnp.concatenate([xd[own, 0:1024], mine, unit.astype(F32).astype(BF16)], axis=0)
    v = coef_a * stack.astype(F32) + dot(stack, p0[...])
    v = coef_a * v + dot(v.astype(BF16), p1[...])
    v = coef_a * v + dot(v.astype(BF16), p2[...])

    def by_gram(v):
        v = dot((coef_a * v + dot(v.astype(BF16), p2[...])).astype(BF16), gh[...])
        return coef_a * v + dot(v.astype(BF16), p2[...])

    next(gathered)
    once = by_gram(v)
    v = coef_a * v + coef_b * once + coef_c * by_gram(once)
    for _ in gathered:
        pass
    x_out[...] = (root * v[0:128]).astype(BF16)
    cross = v[128:160] + lax.dot_general(
        v[160:192].astype(BF16), cfin[...].reshape(1024, 1024), (((1,), (1,)), ((), ())),
        preferred_element_type=F32)
    dual_out[...] = d_v[pl.ds(pl.multiple_of(32 * share, 32), 32), :] - (16.0 * root) * cross

    for copy in stats + lines + pairs + ended:
        copy.wait_send()


def step_of(gradient, weight, dual, threshold):
    vmem = lambda *s: pltpu.VMEM(s, F32)
    half = lambda *s: pltpu.VMEM(s, BF16)

    def bufs(kind, width):
        first, second = kind(3, 64, width), kind(3, 16, width)
        return [first, first, kind(4, 16, width), kind(4, 16, width), second, second]

    n_copies = 38 + 4 + 12 * 2 + 20 * 3
    return pl.pallas_call(
        lambda *refs: kernel(threshold, *refs),
        out_shape=(jax.ShapeDtypeStruct((128, 1024), BF16),
                   jax.ShapeDtypeStruct((32, 1024), F32)),
        in_specs=[pl.BlockSpec(memory_space=pltpu.HBM)] * 3,
        out_specs=[pl.BlockSpec(memory_space=pltpu.VMEM)] * 2,
        scratch_shapes=[
            vmem(128, 1024), vmem(128, 1024), vmem(1024, 1024), half(256, 1024), vmem(128, 1024),
            vmem(128, 1024), vmem(128, 1024), vmem(2, 1, 128), vmem(38, 1, 128), half(256, 1536), half(256, 1024),
            half(8, 2, 2, 2, 16, 1024),
            vmem(4, 64, WIN), vmem(4, 64, WIN), half(4, 2, 2, 4, 16, WIN), half(4, 2, 2, 4, 16, WIN),
            vmem(1024, 1024), half(1024, 1024), half(1024, 1024), half(1024, 1024), half(1024, 1024),
            half(1024, 1024), vmem(1024, 1024), half(1024, 1024),
            half(4, 64, 1024), half(4, 64, 1024), half(4, 4, 2, 2, 16, 1024),
            bufs(vmem, WIN), bufs(half, 1024),
            pltpu.SemaphoreType.DMA((3,)), pltpu.SemaphoreType.DMA((n_copies,)),
            pltpu.SemaphoreType.DMA((n_copies,)),
        ],
        compiler_params=pltpu.CompilerParams(
            collective_id=0, has_side_effects=True, vmem_limit_bytes=59000 * 1024),
        name="step",
    )(gradient, weight, dual)


def finish(width_root, x_ref, d_ref, update_ref, dual_ref):
    update_ref[...] = width_root * x_ref[...].astype(F32)
    dual_ref[...] = d_ref[...]


def local(gradient, weight, dual):
    local_rows, col_count = gradient.shape[1:]
    threshold = 0.5 * math.sqrt(
        local_rows * lax.axis_size(ROW) * col_count * lax.axis_size("grp"))
    iterate, dual_next = step_of(gradient[0], weight[0], dual[0], threshold)
    update, dual_next = pl.pallas_call(
        functools.partial(finish, math.sqrt(col_count)),
        out_shape=(jax.ShapeDtypeStruct((local_rows, col_count), F32),
                   jax.ShapeDtypeStruct(dual_next.shape, F32)),
        name="finish",
    )(iterate, dual_next)
    return (update[None], dual_next[None])


def solution(mesh):
    torus = Mesh(
        mesh.devices.reshape(mesh.shape["grp"], 4, 4, 2), ("grp", "row_0", "row_1", "row_2")
    )
    in_specs = (P("grp", ROW, None), P("grp", ROW, None), P("grp", None, None))
    out_specs = (P("grp", ROW, None), P("grp", ROW, None))
    return jax.shard_map(local, mesh=torus, in_specs=in_specs, out_specs=out_specs, check_vma=False)
```

```python
import functools
import math

import jax
import jax.numpy as jnp
from jax import lax
from jax.experimental import pallas as pl
from jax.experimental.pallas import tpu as pltpu
from jax.sharding import Mesh
from jax.sharding import PartitionSpec as P

ROW = ("row_0", "row_1", "row_2")
MESH = pl.DeviceIdType.MESH
coef_a = 3.4445
coef_b = -4.775
coef_c = 2.0315
epsilon = 1e-06
WIN = 640
STEPS = {4: (0,), 8: (1,), 16: (1, 2), 23: (2,)}
F32 = jnp.float32
BF16 = jnp.bfloat16


class Copies:
    def __init__(self, send, recv):
        self.send, self.recv, self.n = send, recv, 0

    def __call__(self, src, dst, where):
        i = self.n
        self.n += 1
        copy = pltpu.make_async_remote_copy(
            src_ref=src, dst_ref=dst, send_sem=self.send.at[i], recv_sem=self.recv.at[i],
            device_id=where, device_id_type=MESH,
        )
        copy.start()
        return copy


def turn(p, d, n):
    return lax.rem(p + d, n)


class Sum:
    def __init__(self, copies, axis, p, part, arrived, dist=(2, 1, 3)):
        self.copies, self.axis = copies, axis
        self.p, self.part, self.arrived = p, part, arrived
        self.sent = []
        self.send(dist)

    def send(self, dist):
        for d in dist:
            to = turn(self.p, d, 4)
            self.sent.append(
                self.copies(self.part.at[to], self.arrived.at[d - 1], {self.axis: to}))

    def total(self):
        for copy in self.sent:
            copy.wait_recv()
        out = self.part[self.p].astype(F32)
        for d in range(3):
            out += self.arrived[d].astype(F32)
        return out


class Spread:
    def __init__(self, copies, axis, p, at):
        self.sent = [copies(at(p), at(p), {axis: turn(p, d, 4)}) for d in (2, 1, 3)]
        self.came = [at(turn(p, 4 - d, 4)) for d in (2, 1, 3)]

    def each(self):
        for copy, ref in ((self.sent[i], self.came[i]) for i in (1, 2, 0)):
            copy.wait_recv()
            yield ref


def reduce_steps(c, x, y, parts_a, parts_b, bufs, put_a, put_b, sent, split=False):
    ra, rb, qa, qb, ra2, rb2 = bufs
    dtype = qa.dtype
    first = (2,) if split else (2, 1, 3)
    sum_a = Sum(c, "row_1", x, parts_a, ra, first)
    sum_b = Sum(c, "row_0", y, parts_b, rb, first)
    yield
    if split:
        sum_a.send((1, 3))
        sum_b.send((1, 3))
        yield
    va = sum_a.total().astype(dtype)
    for j in range(4):
        qa[j] = va[16 * j:16 * j + 16]
    sum_a2 = Sum(c, "row_0", y, qa, ra2)
    vb = sum_b.total().astype(dtype)
    for j in range(4):
        qb[j] = vb[16 * j:16 * j + 16]
    sum_b2 = Sum(c, "row_1", x, qb, rb2)
    yield
    put_a(sum_a2.total())
    put_b(sum_b2.total())
    for phase in (sum_a, sum_b, sum_a2, sum_b2):
        sent += phase.sent


def gather_steps(c, x, y, k, near_at, far_at, sent):
    near_a, near_b = near_at
    far_a, far_b = far_at
    shared = []

    def pair(ref):
        shared.append(c(ref, ref, {"row_2": 1 - k}))

    na = Spread(c, "row_0", y, near_a)
    nb = Spread(c, "row_1", x, near_b)
    yield
    for _ in na.each():
        pass
    fa = Spread(c, "row_1", x, far_a)
    for _ in nb.each():
        pass
    fb = Spread(c, "row_0", y, far_b)
    pair(far_a(x))
    pair(far_b(y))
    yield
    for refs in zip(fa.each(), fb.each()):
        for ref in refs:
            pair(ref)
    yield
    for copy in shared:
        copy.wait_recv()
    for phase in (na, nb, fa, fb):
        sent += phase.sent
    sent += shared


def kernel(threshold, g_hbm, w_hbm, d_hbm, x_out, dual_out,
           g_ref, w_v, d_v, wst, wt, wt2, g2, stat_s, stat_r, xd, wd, cp, pa, pb, fin, fil, gf, gh, gl, p0, p1, p2, uf, ub,
           ca, cb, cfin, bufs_g, bufs_c, in_sem, send, recv):
    z = lax.axis_index("grp")
    y = lax.axis_index("row_0")
    x = lax.axis_index("row_1")
    k = lax.axis_index("row_2")
    other = 1 - k
    c = Copies(send, recv)
    load_d = pltpu.make_async_copy(d_hbm, d_v, in_sem.at[0])
    load_w = pltpu.make_async_copy(w_hbm, w_v, in_sem.at[1])
    load_g = pltpu.make_async_copy(g_hbm, g_ref, in_sem.at[2])
    load_g.start()
    load_w.start()
    load_d.start()

    barrier = pltpu.get_barrier_semaphore()
    partner = {"row_2": other}
    plane = [{"row_0": turn(y, e, 4), "row_1": turn(x, d, 4), "row_2": turn(k, f, 2)}
             for e in range(4) for d in range(4) for f in range(2) if (e, d, f) != (0, 0, 0)]
    line = [{"grp": turn(z, d, 8)} for d in range(1, 8)]
    for peer in plane + line:
        pl.semaphore_signal(barrier, inc=1, device_id=peer, device_id_type=MESH)

    load_g.wait()
    g = g_ref[...]
    total = jnp.full((1, 128), jnp.sum(g * g), F32)
    stat_s[0] = total
    own = pl.ds(pl.multiple_of(128 * k, 128), 128)
    theirs = pl.ds(pl.multiple_of(128 * other, 128), 128)
    pl.semaphore_wait(barrier, len(plane) + len(line))
    stats = [c(stat_s.at[0], stat_r.at[i], peer) for i, peer in enumerate(plane)]
    pairs = [c(g_ref, g2, partner)]
    load_w.wait()
    w = w_v[...]
    wh = w.astype(BF16)
    wst[0:128] = wh
    wst[128:256] = (w - wh.astype(F32)).astype(BF16)
    wd[own] = wh
    pairs.append(c(wd.at[own], wd.at[own], partner))
    load_d.wait()

    def split(v):
        vh = v.astype(BF16)
        return vh, (v - vh.astype(F32)).astype(BF16)

    def weighted_chunk(j):
        cols = pl.ds(256 * j, 256)
        dh, dl = split(d_v[:, cols])
        both = jnp.dot(wst[...], dh, preferred_element_type=F32)
        acc = both[:128] + both[128:] + jnp.dot(wst[0:128], dl, preferred_element_type=F32)
        dh, dl = split(d_v[cols, :])
        dims = (((1,), (1,)), ((), ()))
        both = lax.dot_general(wst[...], dh, dims, preferred_element_type=F32)
        acc += both[:128] + both[128:]
        acc += lax.dot_general(wst[0:128], dl, dims, preferred_element_type=F32)
        wt[:, cols] = 0.5 * acc

    def half_weighted(m):
        for n in (2 * m, 2 * m + 1):
            weighted_chunk(n)
        cols = pl.ds(512 * m, 512)
        pairs.append(c(wt.at[:, cols], wt2.at[:, cols], partner))

    half_weighted(0)
    for i, copy in enumerate(stats):
        copy.wait_recv()
        total += stat_r[i]
    stat_s[1] = total
    lines = [c(stat_s.at[1], stat_r.at[31 + i], peer) for i, peer in enumerate(line)]
    half_weighted(1)
    for copy in pairs:
        copy.wait_recv()
    for i, copy in enumerate(lines):
        copy.wait_recv()
        total += stat_r[31 + i]

    clip = jnp.minimum(1.0, threshold * lax.rsqrt(total[0:1, 0:1]))
    for rows, ga, wa in ((own, g_ref, wt), (theirs, g2, wt2)):
        t = (clip * ga[...] + wa[...]).astype(BF16)
        xd[rows, 0:1024] = t
        xd[rows, 1024:1536] = t[:, 0:512]

    tn = (((0,), (0,)), ((), ()))
    for i in range(4):
        at = pl.multiple_of(128 * (2 * i + k), 128)
        part = lax.dot_general(
            xd[:, pl.ds(at, 128)], xd[:, pl.ds(at, WIN)], tn, preferred_element_type=F32)
        pa[i] = part[:64]
        pb[i] = part[64:]

    ended = []

    def put_gram(at_hi, at_lo):
        def put(v):
            hi = v.astype(BF16)
            at_hi[...] = hi
            at_lo[...] = (v - hi.astype(F32)).astype(BF16)
        return put

    near = lambda f: (lambda j: f.at[x, k, 0, j], lambda j: f.at[y, k, 1, j])
    far = lambda f: (lambda i: f.at[i, k, 0], lambda i: f.at[i, k, 1])
    gram_steps = reduce_steps(c, x, y, pa, pb, bufs_g,
                              put_gram(near(fin)[0](y), near(fil)[0](y)),
                              put_gram(near(fin)[1](x), near(fil)[1](x)), ended)
    next(gram_steps)
    for b in range(8):
        part = lax.dot_general(
            wd[:, 128 * b:128 * b + 128], xd[:, 0:1024], tn, preferred_element_type=F32)
        cp[b] = part.astype(BF16).reshape(2, 2, 2, 16, 1024)
    for e in range(4):
        for d in range(4):
            ca[d, 16 * e:16 * e + 16] = cp[2 * e + d // 2, d % 2, k, 0]
            cb[e, 16 * d:16 * d + 16] = cp[2 * e + d // 2, d % 2, k, 1]
    next(gram_steps)

    def put_at(ref):
        def put(v):
            ref[...] = v.astype(BF16)
        return put

    product_near = (lambda j: cfin.at[j, x, k, 0], lambda j: cfin.at[y, j, k, 1])
    product_far = (lambda i: cfin.at[:, i, k, 0], lambda i: cfin.at[i, :, k, 1])
    reduced = reduce_steps(c, x, y, ca, cb, bufs_c, put_at(product_near[0](y)),
                           put_at(product_near[1](x)), ended, True)
    gathered = gather_steps(c, x, y, k, product_near, product_far, ended)
    for _ in gram_steps:
        pass
    high = gather_steps(c, x, y, k, near(fin), far(fin), ended)
    low = gather_steps(c, x, y, k, near(fil), far(fil), ended)
    next(high)
    next(low)
    next(high)
    next(low)
    next(reduced)
    next(reduced)
    for _ in high:
        pass

    trace = jnp.zeros((1, 1), F32)
    eye = (lax.broadcasted_iota(jnp.int32, (128, 128), 0)
           == lax.broadcasted_iota(jnp.int32, (128, 128), 1))
    for b in range(8):
        i, core = b // 2, b % 2
        for j in range(5):
            m = (b + j) % 8
            block = fin[i, core, :, :, :, 128 * j:128 * j + 128].reshape(128, 128)
            rows, cols = pl.ds(128 * b, 128), pl.ds(128 * m, 128)
            gh[rows, cols] = block
            if j == 0:
                trace += jnp.sum(jnp.where(eye, block.astype(F32), 0.0), keepdims=True)
            if 0 < j < 4:
                gh[cols, rows] = block.T
    scale = 1.0 / (trace + epsilon)
    root = jnp.sqrt(scale)

    def dot(u, v):
        return jnp.dot(u, v, preferred_element_type=F32)

    TILE = 256
    tiles = [pl.ds(TILE * n, TILE) for n in range(1024 // TILE)]
    done = [0]

    def advance():
        done[0] += 1
        for steps in STEPS.get(done[0], ()):
            next((low, reduced, gathered)[steps], None)

    def mirror(ref, t, v):
        for m in range(1, v.shape[0] // TILE):
            ref[tiles[t], pl.ds(TILE * (t + m), TILE)] = v[TILE * m:TILE * m + TILE].T

    def square(p, t, s):
        rows, n = pl.ds(TILE * t, 1024 - TILE * t), tiles[t]
        g = gh[rows, n].astype(F32) if p is p0 else gf[rows, n]
        v = ((coef_b * s) * g + (coef_c * s * s) * dot(gh[rows, :], gh[:, n])).astype(BF16)
        p[rows, n] = v
        mirror(p, t, v)
        advance()

    def left(p, n):
        g = gh[:, n].astype(F32) if p is p0 else gf[:, n]
        u = coef_a * g + dot(p[...], gh[:, n])
        uf[:, n] = u
        ub[:, n] = u.astype(BF16)
        advance()

    def right(p, n, s):
        v = coef_a * uf[:, n] + dot(ub[...], p[:, n])
        if p is p0:
            v = s * (v + (coef_a * coef_a) * gl[:, n].astype(F32))
        gf[:, n] = v
        gh[:, n] = v.astype(BF16)
        advance()

    for t in range(len(tiles)):
        square(p0, t, scale)
    for n in tiles:
        left(p0, n)
    for _ in low:
        pass
    for b in range(8):
        i, core = b // 2, b % 2
        for j in range(5):
            m = (b + j) % 8
            block = fil[i, core, :, :, :, 128 * j:128 * j + 128].reshape(128, 128)
            rows, cols = pl.ds(128 * b, 128), pl.ds(128 * m, 128)
            gl[rows, cols] = block
            if 0 < j < 4:
                gl[cols, rows] = block.T
    for n in tiles:
        right(p0, n, scale)
    for t in range(len(tiles)):
        square(p1, t, 1.0)
    for n in tiles:
        left(p1, n)
    for t in range(len(tiles)):
        rows, n = pl.ds(TILE * t, 1024 - TILE * t), tiles[t]
        v = coef_a * uf[rows, n] + dot(ub[rows, :], p1[:, n])
        gf[rows, n] = v
        gh[rows, n] = v.astype(BF16)
        mirror(gh, t, v.astype(BF16))
        advance()
    for t in range(len(tiles)):
        square(p2, t, 1.0)

    mine = cfin[y, x, k].reshape(32, 1024)
    share = 8 * y + 2 * x + k
    unit = (lax.broadcasted_iota(jnp.int32, (32, 1024), 0) + 32 * share
            == lax.broadcasted_iota(jnp.int32, (32, 1024), 1))
    stack = jnp.concatenate([xd[own, 0:1024], mine, unit.astype(F32).astype(BF16)], axis=0)
    v = coef_a * stack.astype(F32) + dot(stack, p0[...])
    v = coef_a * v + dot(v.astype(BF16), p1[...])
    v = coef_a * v + dot(v.astype(BF16), p2[...])

    def by_gram(v):
        v = dot((coef_a * v + dot(v.astype(BF16), p2[...])).astype(BF16), gh[...])
        return coef_a * v + dot(v.astype(BF16), p2[...])

    next(gathered)
    once = by_gram(v)
    v = coef_a * v + coef_b * once + coef_c * by_gram(once)
    for _ in gathered:
        pass
    x_out[...] = (root * v[0:128]).astype(BF16)
    cross = v[128:160] + lax.dot_general(
        v[160:192].astype(BF16), cfin[...].reshape(1024, 1024), (((1,), (1,)), ((), ())),
        preferred_element_type=F32)
    dual_out[...] = d_v[pl.ds(pl.multiple_of(32 * share, 32), 32), :] - (16.0 * root) * cross

    for copy in stats + lines + pairs + ended:
        copy.wait_send()


def step_of(gradient, weight, dual, threshold):
    vmem = lambda *s: pltpu.VMEM(s, F32)
    half = lambda *s: pltpu.VMEM(s, BF16)

    def bufs(kind, width):
        first, second = kind(3, 64, width), kind(3, 16, width)
        return [first, first, kind(4, 16, width), kind(4, 16, width), second, second]

    n_copies = 38 + 4 + 12 * 2 + 20 * 3
    return pl.pallas_call(
        lambda *refs: kernel(threshold, *refs),
        out_shape=(jax.ShapeDtypeStruct((128, 1024), BF16),
                   jax.ShapeDtypeStruct((32, 1024), F32)),
        in_specs=[pl.BlockSpec(memory_space=pltpu.HBM)] * 3,
        out_specs=[pl.BlockSpec(memory_space=pltpu.VMEM)] * 2,
        scratch_shapes=[
            vmem(128, 1024), vmem(128, 1024), vmem(1024, 1024), half(256, 1024), vmem(128, 1024),
            vmem(128, 1024), vmem(128, 1024), vmem(2, 1, 128), vmem(38, 1, 128), half(256, 1536), half(256, 1024),
            half(8, 2, 2, 2, 16, 1024),
            vmem(4, 64, WIN), vmem(4, 64, WIN), half(4, 2, 2, 4, 16, WIN), half(4, 2, 2, 4, 16, WIN),
            vmem(1024, 1024), half(1024, 1024), half(1024, 1024), half(1024, 1024), half(1024, 1024),
            half(1024, 1024), vmem(1024, 1024), half(1024, 1024),
            half(4, 64, 1024), half(4, 64, 1024), half(4, 4, 2, 2, 16, 1024),
            bufs(vmem, WIN), bufs(half, 1024),
            pltpu.SemaphoreType.DMA((3,)), pltpu.SemaphoreType.DMA((n_copies,)),
            pltpu.SemaphoreType.DMA((n_copies,)),
        ],
        compiler_params=pltpu.CompilerParams(
            collective_id=0, has_side_effects=True, vmem_limit_bytes=59000 * 1024),
        name="step",
    )(gradient, weight, dual)


def finish(width_root, x_ref, d_ref, update_ref, dual_ref):
    update_ref[...] = width_root * x_ref[...].astype(F32)
    dual_ref[...] = d_ref[...]


def local(gradient, weight, dual):
    local_rows, col_count = gradient.shape[1:]
    threshold = 0.5 * math.sqrt(
        local_rows * lax.axis_size(ROW) * col_count * lax.axis_size("grp"))
    iterate, dual_next = step_of(gradient[0], weight[0], dual[0], threshold)
    update, dual_next = pl.pallas_call(
        functools.partial(finish, math.sqrt(col_count)),
        out_shape=(jax.ShapeDtypeStruct((local_rows, col_count), F32),
                   jax.ShapeDtypeStruct(dual_next.shape, F32)),
        name="finish",
    )(iterate, dual_next)
    return (update[None], dual_next[None])


def solution(mesh):
    torus = Mesh(
        mesh.devices.reshape(mesh.shape["grp"], 4, 4, 2), ("grp", "row_0", "row_1", "row_2")
    )
    in_specs = (P("grp", ROW, None), P("grp", ROW, None), P("grp", None, None))
    out_specs = (P("grp", ROW, None), P("grp", ROW, None))
    return jax.shard_map(local, mesh=torus, in_specs=in_specs, out_specs=out_specs, check_vma=False)
```
